32 devices in a mesh: dom: 8 (over z, core), group: 4 (over y, x).
Axes of the slice: x: 2, y: 2, z: 4, core: 2. Of those that a mesh axis runs over, the one named last changes fastest.
Arguments:
- start: bfloat16 [64, 32768], P(None, ('dom', 'group')), may hold values from -8.1 to 8.1
- tiles: int32 [32, 32, 128, 128], P(('dom', 'group')), may hold values from 0 to 15
- row_ptr: int32 [32, 9], P(('dom', 'group')), may hold values from 0 to 32, as said below
- col_part: int32 [32, 32], P(('dom', 'group')), may hold values from 0 to 7
- col_local: int32 [32, 32], P(('dom', 'group')), may hold values from 0 to 31, as said below
- halo_list: int32 [8, 8, 4], P('dom'), may hold values from 0 to 31
Outputs:
- vectors: bfloat16 [64, 32768], P(None, ('dom', 'group'))
- ritz: float32 [64, 64], replicated
The draws below stay inside these ranges and needn't reach their ends.
Inputs may be any that keep to these rules, and one draw needn't show every extreme that they name: `row_ptr`: each row is strictly increasing from 0, so every block row has one or more slots; its last entry is at most 32 and equals 32 on some device row. `col_local`: below 32 where col_part names the row's own partition, below 4 otherwise.
All inputs are finite; a program needn't handle non-finite values.
Results may differ from the reference program's by a relative error of at most 0.012.
Values may be sent and summed in bfloat16 or wider, within the bound.
A program may use at most 64 MiB of HBM per device.

```python
import math
import jax
import jax.numpy as jnp
from jax import lax

BLOCK = 128
K = 64
BR_DEV = 8
ITERS = 2
HALO = 4
SLOTS = 32
PARTITIONS = 8
SUBSHARDS = 4
NBP = 32
NB = 256
ROWS = 32768
N_DOM = 8
N_GROUP = 4


def draw_start(key, part):
    first, second, third, fourth = jax.random.split(jax.random.fold_in(key, 37), 4)
    shared = jnp.clip(jax.random.normal(first, (1, ROWS), jnp.float32), -3.0, 3.0)
    noise = jnp.clip(jax.random.normal(second, (K, ROWS), jnp.float32), -3.0, 3.0)
    scale = jnp.exp(jax.random.uniform(third, (K, 1), jnp.float32, math.log(0.5), math.log(2.0)))
    spread = 0.6
    sign = jnp.where(jax.random.randint(fourth, (K, 1), 0, 2) == 0, -1.0, 1.0).astype(jnp.float32)
    return (sign * scale * shared + spread * noise).astype(jnp.bfloat16)


def draw_row_ptr(key, part):
    first, second, third = jax.random.split(jax.random.fold_in(key, 11), 3)
    count = PARTITIONS * SUBSHARDS
    used = jax.random.randint(first, (count,), SLOTS // 4, SLOTS + 1)
    fullest = jax.random.randint(second, (), 0, count)
    used = jnp.where(jnp.arange(count) == fullest, SLOTS, used)
    spread = used // (8 * BR_DEV)
    noise = jax.random.randint(third, (count, BR_DEV - 1), 0, 1 << 20)
    jitter = noise % (2 * spread[:, None] + 1) - spread[:, None]
    inner = jnp.arange(1, BR_DEV)[None, :] * used[:, None] // BR_DEV + jitter
    zeros = jnp.zeros((count, 1), jnp.int32)
    return jnp.concatenate([zeros, inner.astype(jnp.int32), used[:, None].astype(jnp.int32)], axis=1).astype(jnp.int32)


def link_draw(key):
    first, second, third, fourth = jax.random.split(jax.random.fold_in(key, 23), 4)
    count = PARTITIONS * SUBSHARDS
    own = (jnp.arange(count, dtype=jnp.int32) // SUBSHARDS)[:, None]
    remote = jax.random.randint(first, (count, SLOTS), 0, 4) == 0
    other = (own + jax.random.randint(second, (count, SLOTS), 1, PARTITIONS)) % PARTITIONS
    parts = jnp.where(remote, other, own).astype(jnp.int32)
    places = jnp.where(remote, jax.random.randint(third, (count, SLOTS), 0, HALO), jax.random.randint(fourth, (count, SLOTS), 0, NBP))
    return (parts, places.astype(jnp.int32))


def draw_col_part(key, part):
    return link_draw(key)[0]


def draw_col_local(key, part):
    return link_draw(key)[1]


def plant(values, stream_key, low, top_value):
    longest = values.shape.index(max(values.shape))
    spots = []
    for shift in (0, 1):
        where = [jax.random.randint(jax.random.fold_in(stream_key, axis), (), 0, length) for axis, length in enumerate(values.shape)]
        where[longest] = (where[longest] + shift) % values.shape[longest]
        spots.append(tuple(where))
    return values.at[spots[0]].set(low).at[spots[1]].set(top_value)


def setup_inputs(seed: int = 0) -> dict:
    splits = jax.random.split(jax.random.key(seed), 7)
    return {
        "start": draw_start(jax.random.fold_in(splits[6], 71), 0),
        "tiles": plant(jax.random.randint(splits[1], (N_DOM * N_GROUP, SLOTS, BLOCK, BLOCK), 0, 16), jax.random.fold_in(splits[1], 1), 0, 15).astype(jnp.int32),
        "row_ptr": draw_row_ptr(jax.random.fold_in(splits[6], 71), 0),
        "col_part": draw_col_part(jax.random.fold_in(splits[6], 71), 0),
        "col_local": draw_col_local(jax.random.fold_in(splits[6], 71), 0),
        "halo_list": plant(jax.random.randint(splits[5], (N_DOM, N_DOM, HALO), 0, NBP), jax.random.fold_in(splits[5], 1), 0, NBP - 1).astype(jnp.int32),
    }


def apply_graph(vectors, tiles, row_ptr, col_part, col_local, halo_list):
    blocked = vectors.astype(jnp.float32).reshape(K, NB, BLOCK)

    def one_row(entry):
        own = entry // SUBSHARDS
        pointers = row_ptr[entry]
        parts = col_part[entry]
        places = col_local[entry]
        remote = halo_list[parts, own, jnp.clip(places, 0, HALO - 1)]
        column = jnp.where(parts == own, own * NBP + places, parts * NBP + remote).astype(jnp.int32)
        picked = jnp.take(blocked, column, axis=1)
        centred = tiles[entry].astype(jnp.float32) - 7.5
        products = jnp.einsum('ksj,sij->ksi', picked, centred, precision=lax.Precision.HIGHEST)
        slot_ids = jnp.arange(SLOTS, dtype=jnp.int32)
        member = ((slot_ids[None, :] >= pointers[:-1, None]) & (slot_ids[None, :] < pointers[1:, None])).astype(jnp.float32)
        summed = jnp.einsum('rs,ksi->kri', member, products, precision=lax.Precision.HIGHEST)
        counts = (pointers[1:] - pointers[:-1]).astype(jnp.float32)
        return summed * (1.0 / (4.0 * jnp.sqrt(BLOCK * counts)))[None, :, None]
    result = lax.map(one_row, jnp.arange(PARTITIONS * SUBSHARDS, dtype=jnp.int32))
    return jnp.transpose(result, (1, 0, 2, 3)).reshape(K, ROWS)

def reference(start, tiles, row_ptr, col_part, col_local, halo_list):
    vectors = start
    for step in range(ITERS):
        image = apply_graph(vectors, tiles, row_ptr, col_part, col_local, halo_list)
        rounded = image.astype(jnp.bfloat16)
        gram = jnp.dot(rounded.astype(jnp.float32), rounded.T.astype(jnp.float32), preferred_element_type=jnp.float32) / ROWS
        lower = jnp.linalg.cholesky(gram)
        vectors = lax.linalg.triangular_solve(lower, rounded.astype(jnp.float32), left_side=True, lower=True).astype(jnp.bfloat16)
    final = apply_graph(vectors, tiles, row_ptr, col_part, col_local, halo_list)
    ritz = jnp.dot(vectors.astype(jnp.float32), final.T, precision=lax.Precision.HIGHEST) / ROWS
    return (vectors, ritz)
```

```python
import functools

import jax
import jax.numpy as jnp
from jax import lax
from jax.experimental import pallas as pl
from jax.experimental.pallas import tpu as pltpu
from jax.sharding import PartitionSpec as P

ITERS = 2
MESH = pl.DeviceIdType.MESH
HIGH = lax.Precision.HIGH
HIGHEST = lax.Precision.HIGHEST
CHUNK = 8
PANEL = 4
ROWS = 16
LAG = 2


def dot(a, b, dims=((1,), (0,)), precision=None):
    return lax.dot_general(a, b, (dims, ((), ())), precision=precision, preferred_element_type=jnp.float32)


def factor_start(gram):
    k = gram.shape[0]
    rows = lax.broadcasted_iota(jnp.int32, (k, k), 0)
    cols = lax.broadcasted_iota(jnp.int32, (k, k), 1)
    work = jnp.concatenate([gram, jnp.where(rows == cols, 1.0, 0.0).astype(jnp.float32)], axis=1)
    return work, jnp.ones(work.shape, jnp.float32)


def factor_steps(state, first, last):
    work, pivots = state
    row_ids = lax.broadcasted_iota(jnp.int32, work.shape, 0)
    for i in range(first, last, PANEL):
        cols = [jnp.broadcast_to(work[:, i + b : i + b + 1], work.shape) for b in range(PANEL)]
        rows = [work[i + b : i + b + 1, :] for b in range(PANEL)]
        for b in range(PANEL):
            pivot = cols[b][i + b : i + b + 1, :]
            inv = 1.0 / pivot
            pivots = jnp.where(row_ids == i + b, pivot, pivots)
            for c in range(b + 1, PANEL):
                ratio = cols[c][i + b : i + b + 1, :] * inv
                rows[c] = rows[c] - (cols[b][i + c : i + c + 1, :] * inv) * rows[b]
                cols[c] = cols[c] - cols[b] * ratio
            work = work - jnp.where(row_ids > i + b, cols[b], 0.0) * (rows[b] * inv)
    return work, pivots


def factor_end(state):
    work, pivots = state
    k = work.shape[0]
    return work[:, k:] * (1.0 / jnp.sqrt(pivots[:, k:]))


def kernel(n_dom, n_group, halo, total_rows, *refs):
    start_hbm, tiles_ref, ptr_hbm, cpart_hbm, cloc_hbm, halo_hbm, vec_ref, ritz_ref = refs[:8]
    start_ref, ptr_ref, cpart_ref, cloc_ref, halo_ref, in_sem = refs[8:14]
    refs = refs[14:]
    n_apply = ITERS + 1
    n_chunk = start_ref.shape[0] // ROWS
    parts, refs = refs[: n_apply * n_chunk], refs[n_apply * n_chunk :]
    halos, refs = refs[: n_apply * n_chunk], refs[n_apply * n_chunk :]
    stage_ref, raw, tb, prod, near_ref, far_ref, scale_ref, bf_ref, im_ref = refs[:9]
    g_src, g_one, g_two, tile_sem, f_recv, z_recv, x_send, g_recv, g_send = refs[9:]

    def part(a, c):
        return parts[a * n_chunk + c]

    def border(a, c):
        return halos[a * n_chunk + c]

    own = lax.axis_index("dom")
    me = lax.axis_index("group")
    slots, block = tb.shape[0], tb.shape[1]
    width = start_ref.shape[0]
    block_rows = start_ref.shape[1] // block
    in_part = block_rows * n_group
    pair = 2 if n_dom % 2 == 0 else 1
    core = lax.rem(own, pair)
    doms = []
    for step in range(n_dom // 2, 0, -1):
        doms.append(step)
        if n_dom - step != step:
            doms.append(n_dom - step)

    def up(offset):
        return lax.rem(own + offset, n_dom)

    def beside(offset):
        return lax.rem(me + offset, n_group)

    def twin(offset):
        return own - core + lax.rem(core + offset, pair)

    plane = [(i, j) for i in range(pair) for j in range(n_group) if i or j]

    def remote(src, dst, send_sem, recv_sem, device):
        return pltpu.make_async_remote_copy(
            src_ref=src, dst_ref=dst, send_sem=send_sem, recv_sem=recv_sem, device_id=device, device_id_type=MESH
        )

    def take(ref, sem):
        pltpu.make_async_copy(ref, ref, sem).wait()

    smalls = [
        pltpu.make_async_copy(src, dst, in_sem.at[i])
        for i, (src, dst) in enumerate(
            [
                (start_hbm, start_ref),
                (ptr_hbm, ptr_ref),
                (cpart_hbm, cpart_ref),
                (cloc_hbm, cloc_ref),
                (halo_hbm, halo_ref),
            ]
        )
    ]
    for load in smalls:
        load.start()

    barrier = pltpu.get_barrier_semaphore()
    for i, j in plane:
        pl.semaphore_signal(barrier, inc=1, device_id=(twin(i), beside(j)), device_id_type=MESH)
    others = []
    for offset in range(1, n_dom):
        others.append(offset)
    for offset in others:
        pl.semaphore_signal(barrier, inc=1, device_id=(up(offset), me), device_id_type=MESH)

    n_loads = slots // CHUNK
    loads = [
        pltpu.make_async_copy(
            tiles_ref.at[0, pl.ds(c * CHUNK, CHUNK)], raw.at[pl.ds(c * CHUNK, CHUNK)], tile_sem.at[c]
        )
        for c in range(n_loads)
    ]
    for load in loads:
        load.start()

    def put_own(a, c, values):
        for b in range(block_rows):
            part(a, c)[me * block_rows + b] = values[:, b * block : (b + 1) * block]

    def near_start(a, c):
        mine = part(a, c).at[pl.ds(me * block_rows, block_rows)]
        for j in range(1, n_group):
            remote(mine, mine, x_send.at[a, c], f_recv.at[a, c], (own, beside(j))).start()

    def far_start(a, c):
        take(part(a, c).at[pl.ds(0, in_part - block_rows)], f_recv.at[a, c])
        for o in doms:
            for h in range(halo):
                stage_ref[a, c, o, h] = part(a, c)[halo_ref[0, h, up(o)]]
            remote(
                stage_ref.at[a, c, o],
                border(a, c).at[pl.ds(own * halo, halo)],
                x_send.at[a, c],
                z_recv.at[a, c],
                (up(o), me),
            ).start()

    def far_wait(a, c):
        take(border(a, c).at[pl.ds(0, (n_dom - 1) * halo)], z_recv.at[a, c])

    def sends_wait(a, c):
        for _ in range(n_group - 1):
            take(part(a, c).at[pl.ds(0, block_rows)], x_send.at[a, c])
        for o in doms:
            take(stage_ref.at[a, c, o], x_send.at[a, c])

    def apply_graph(a, c):
        def body(g, total):
            for i in range(CHUNK):
                s = g * CHUNK + i
                near = part(a, c)[near_ref[s]]
                far = border(a, c)[far_ref[s]]
                picked = jnp.where(cpart_ref[0, s] == own, near, far)
                total = total + dot(picked, tb[s], ((1,), (1,)))
                prod[s + 1] = total
            return total

        lax.fori_loop(0, slots // CHUNK, body, jnp.zeros((ROWS, block), jnp.float32))
        out = []
        for r in range(block_rows):
            out.append((prod[ptr_ref[0, r + 1]] - prod[ptr_ref[0, r]]) * scale_ref[r : r + 1, :])
        return jnp.concatenate(out, axis=1)

    half = width // pair
    fold = half // 2

    def sum_one(t, value):
        for i in range(pair):
            packed = jnp.concatenate(
                [value[i * half : i * half + fold], value[i * half + fold : (i + 1) * half]], axis=1
            )
            g_src[t, i] = packed
        g_one[t, core * n_group + me] = g_src[t, core]
        for i, j in plane:
            remote(
                g_src.at[t, lax.rem(core + i, pair)],
                g_one.at[t, core * n_group + me],
                g_send.at[t],
                g_recv.at[t, 0],
                (twin(i), beside(j)),
            ).start()

    def sum_two(t):
        take(g_one.at[t, pl.ds(0, len(plane))], g_recv.at[t, 0])
        total = g_one[t, 0]
        for j in range(1, pair * n_group):
            total = total + g_one[t, j]
        g_two[t, own] = total
        for o in doms:
            remote(g_two.at[t, own], g_two.at[t, own], g_send.at[t], g_recv.at[t, 1], (up(o), me)).start()

    def sum_end(t):
        take(g_two.at[t, pl.ds(0, n_dom - 1)], g_recv.at[t, 1])
        pieces = []
        for i in range(pair):
            total = g_two[t, i]
            for j in range(i + pair, n_dom, pair):
                total = total + g_two[t, j]
            pieces += [total[:, :width], total[:, width:]]
        return jnp.concatenate(pieces, axis=0) * (1.0 / total_rows)

    def sum_sends(t):
        for _ in range(len(plane) + n_dom - 1):
            take(g_one.at[t, 0], g_send.at[t])

    smalls[0].wait()
    for c in range(n_chunk):
        put_own(0, c, start_ref[c * ROWS : (c + 1) * ROWS, :])
    pl.semaphore_wait(barrier, len(plane) + len(others))
    for c in range(n_chunk):
        near_start(0, c)
    for load in smalls[1:]:
        load.wait()
    for s in range(slots):
        here = cpart_ref[0, s] == own
        near_ref[s] = jnp.where(here, cloc_ref[0, s], 0)
        far_ref[s] = jnp.where(here, 0, cpart_ref[0, s] * halo + cloc_ref[0, s])
    for r in range(block_rows):
        count = jnp.full((1, block), ptr_ref[0, r + 1] - ptr_ref[0, r], jnp.int32).astype(jnp.float32)
        scale_ref[r : r + 1, :] = 1.0 / (4.0 * jnp.sqrt(block * count))
    prod[0] = jnp.zeros((ROWS, block), jnp.float32)

    def convert_group(c):
        loads[c].wait()

        def convert(i, carry):
            s = c * CHUNK + i
            tb[s] = (raw[s].astype(jnp.float32) - 7.5).astype(jnp.bfloat16)
            return carry

        lax.fori_loop(0, CHUNK, convert, 0)

    for c in range(n_loads // 2):
        convert_group(c)
    for c in range(n_chunk):
        far_start(0, c)
    for c in range(n_loads // 2, n_loads):
        convert_group(c)

    state = {}

    def extra(a, c):
        if a == 1:
            if c == 0:
                state["one"] = None
            if c == 1:
                sum_two(0)
            if c == 3 % n_chunk:
                state["m"] = factor_start(sum_end(0))
                state["m"] = factor_steps(state["m"], 0, width)
                state["m1"] = factor_end(state["m"])
        if a == 2:
            if c == 1:
                sum_two(1)
            if c == 3 % n_chunk:
                g2 = sum_end(1)
                m1 = state["m1"]
                g2 = dot(m1, dot(g2, m1, ((1,), (1,)), precision=HIGHEST), precision=HIGHEST)
                m2 = factor_end(factor_steps(factor_start(g2), 0, width))
                state["m"] = dot(m2, m1, precision=HIGHEST)

    for a in range(n_apply):
        for c in range(n_chunk):
            far_wait(a, c)
            image = apply_graph(a, c)
            if a < ITERS:
                rounded = image.astype(jnp.bfloat16)
                put_own(a + 1, c, rounded)
                near_start(a + 1, c)
                bf_ref[a, c * ROWS : (c + 1) * ROWS, :] = rounded
                if c >= LAG:
                    far_start(a + 1, c - LAG)
            if a >= 1:
                im_ref[a - 1, c * ROWS : (c + 1) * ROWS, :] = image
            extra(a, c)
        if a < ITERS:
            sum_one(a, dot(bf_ref[a], bf_ref[a], ((1,), (1,))))
            for c in range(n_chunk - LAG, n_chunk):
                far_start(a + 1, c)

    local = dot(im_ref[0], im_ref[1], ((1,), (1,)), precision=HIGH)
    sum_one(ITERS, local)
    whole = state["m"]
    vec_ref[...] = dot(whole, im_ref[0], precision=HIGH).astype(jnp.bfloat16)
    sum_two(ITERS)
    for a in range(n_apply):
        for c in range(n_chunk):
            sends_wait(a, c)
    h = sum_end(ITERS)
    ritz_ref[...] = dot(whole, dot(h, whole, ((1,), (1,)), precision=HIGHEST), precision=HIGHEST)
    for t in range(n_apply):
        sum_sends(t)


def finish(vec_in, ritz_in, vec_out, ritz_out):
    vec_out[...] = vec_in[...]
    ritz_out[...] = ritz_in[...]


def solution(mesh):
    n_dom, n_group = mesh.shape["dom"], mesh.shape["group"]
    n_apply = ITERS + 1
    pair = 2 if n_dom % 2 == 0 else 1

    def step(start, tiles, row_ptr, col_part, col_local, halo_list):
        width, rows_dev = start.shape
        slots, block = tiles.shape[1], tiles.shape[2]
        halo = halo_list.shape[2]
        in_part = rows_dev // block * n_group
        halo_list = jnp.transpose(halo_list, (0, 2, 1))
        n_chunk = width // ROWS
        vmem = pl.BlockSpec(memory_space=pltpu.VMEM)
        dma = pltpu.SemaphoreType.DMA
        outs = (
            jax.ShapeDtypeStruct((width, rows_dev), jnp.bfloat16),
            jax.ShapeDtypeStruct((width, width), jnp.float32),
        )
        packed = (width // pair // 2, 2 * width)
        vectors, ritz = pl.pallas_call(
            functools.partial(kernel, n_dom, n_group, halo, rows_dev * n_dom * n_group),
            out_shape=outs,
            in_specs=[pl.BlockSpec(memory_space=pltpu.HBM)] * 6,
            out_specs=(vmem, vmem),
            scratch_shapes=[
                pltpu.VMEM(start.shape, start.dtype),
                pltpu.SMEM(row_ptr.shape, jnp.int32),
                pltpu.SMEM(col_part.shape, jnp.int32),
                pltpu.SMEM(col_local.shape, jnp.int32),
                pltpu.SMEM(halo_list.shape, jnp.int32),
                dma((5,)),
            ]
            + [pltpu.VMEM((in_part, ROWS, block), jnp.bfloat16)] * (n_apply * n_chunk)
            + [pltpu.VMEM((n_dom * halo, ROWS, block), jnp.bfloat16)] * (n_apply * n_chunk)
            + [
                pltpu.VMEM((n_apply, n_chunk, n_dom, halo, ROWS, block), jnp.bfloat16),
                pltpu.VMEM((slots, block, block), jnp.int32),
                pltpu.VMEM((slots, block, block), jnp.bfloat16),
                pltpu.VMEM((slots + 1, ROWS, block), jnp.float32),
                pltpu.SMEM((slots,), jnp.int32),
                pltpu.SMEM((slots,), jnp.int32),
                pltpu.VMEM((rows_dev // block, block), jnp.float32),
                pltpu.VMEM((ITERS, width, rows_dev), jnp.bfloat16),
                pltpu.VMEM((2, width, rows_dev), jnp.float32),
                pltpu.VMEM((n_apply, pair) + packed, jnp.float32),
                pltpu.VMEM((n_apply, pair * n_group) + packed, jnp.float32),
                pltpu.VMEM((n_apply, n_dom) + packed, jnp.float32),
                dma((slots // CHUNK,)),
                dma((n_apply, n_chunk)),
                dma((n_apply, n_chunk)),
                dma((n_apply, n_chunk)),
                dma((n_apply, 2)),
                dma((n_apply,)),
            ],
            compiler_params=pltpu.CompilerParams(
                collective_id=0, has_side_effects=True, vmem_limit_bytes=67043328
            ),
        )(start, tiles, row_ptr, col_part, col_local, halo_list)
        return pl.pallas_call(finish, out_shape=outs, in_specs=[vmem, vmem], out_specs=(vmem, vmem))(vectors, ritz)

    return jax.shard_map(
        step,
        mesh=mesh,
        in_specs=(
            P(None, ("dom", "group")),
            P(("dom", "group"), None, None, None),
            P(("dom", "group"), None),
            P(("dom", "group"), None),
            P(("dom", "group"), None),
            P("dom", None, None),
        ),
        out_specs=(P(None, ("dom", "group")), P()),
        check_vma=False,
    )
```

```python
import functools

import jax
import jax.numpy as jnp
from jax import lax
from jax.experimental import pallas as pl
from jax.experimental.pallas import tpu as pltpu
from jax.sharding import PartitionSpec as P

ITERS = 2
MESH = pl.DeviceIdType.MESH
HIGH = lax.Precision.HIGH
HIGHEST = lax.Precision.HIGHEST
CHUNK = 8
PANEL = 4
ROWS = 16
LAG = 1


def dot(a, b, dims=((1,), (0,)), precision=None):
    return lax.dot_general(a, b, (dims, ((), ())), precision=precision, preferred_element_type=jnp.float32)


def factor_start(gram):
    k = gram.shape[0]
    rows = lax.broadcasted_iota(jnp.int32, (k, k), 0)
    cols = lax.broadcasted_iota(jnp.int32, (k, k), 1)
    work = jnp.concatenate([gram, jnp.where(rows == cols, 1.0, 0.0).astype(jnp.float32)], axis=1)
    return work, jnp.ones(work.shape, jnp.float32)


def factor_steps(state, first, last):
    work, pivots = state
    row_ids = lax.broadcasted_iota(jnp.int32, work.shape, 0)
    for i in range(first, last, PANEL):
        cols = [jnp.broadcast_to(work[:, i + b : i + b + 1], work.shape) for b in range(PANEL)]
        rows = [work[i + b : i + b + 1, :] for b in range(PANEL)]
        for b in range(PANEL):
            pivot = cols[b][i + b : i + b + 1, :]
            inv = 1.0 / pivot
            pivots = jnp.where(row_ids == i + b, pivot, pivots)
            for c in range(b + 1, PANEL):
                ratio = cols[c][i + b : i + b + 1, :] * inv
                rows[c] = rows[c] - (cols[b][i + c : i + c + 1, :] * inv) * rows[b]
                cols[c] = cols[c] - cols[b] * ratio
            work = work - jnp.where(row_ids > i + b, cols[b], 0.0) * (rows[b] * inv)
    return work, pivots


def factor_end(state):
    work, pivots = state
    k = work.shape[0]
    return work[:, k:] * (1.0 / jnp.sqrt(pivots[:, k:]))


def kernel(n_dom, n_group, halo, total_rows, *refs):
    start_hbm, tiles_ref, ptr_hbm, cpart_hbm, cloc_hbm, halo_hbm, vec_ref, ritz_ref = refs[:8]
    start_ref, ptr_ref, cpart_ref, cloc_ref, halo_ref, in_sem = refs[8:14]
    refs = refs[14:]
    n_apply = ITERS + 1
    n_chunk = start_ref.shape[0] // ROWS
    parts, refs = refs[: n_apply * n_chunk], refs[n_apply * n_chunk :]
    halos, refs = refs[: n_apply * n_chunk], refs[n_apply * n_chunk :]
    stage_ref, raw, tb, prod, near_ref, far_ref, scale_ref, bf_ref, im_ref = refs[:9]
    g_src, g_one, g_two, tile_sem, f_recv, z_recv, x_send, g_recv, g_send = refs[9:]

    def part(a, c):
        return parts[a * n_chunk + c]

    def border(a, c):
        return halos[a * n_chunk + c]

    own = lax.axis_index("dom")
    me = lax.axis_index("group")
    slots, block = raw.shape[0], raw.shape[1]
    width = start_ref.shape[0]
    block_rows = start_ref.shape[1] // block
    in_part = block_rows * n_group
    pair = 2 if n_dom % 2 == 0 else 1
    core = lax.rem(own, pair)
    doms = []
    for step in range(n_dom // 2, 0, -1):
        doms.append(step)
        if n_dom - step != step:
            doms.append(n_dom - step)

    def up(offset):
        return lax.rem(own + offset, n_dom)

    def beside(offset):
        return lax.rem(me + offset, n_group)

    def twin(offset):
        return own - core + lax.rem(core + offset, pair)

    plane = [(i, j) for i in range(pair) for j in range(n_group) if i or j]

    def remote(src, dst, send_sem, recv_sem, device):
        return pltpu.make_async_remote_copy(
            src_ref=src, dst_ref=dst, send_sem=send_sem, recv_sem=recv_sem, device_id=device, device_id_type=MESH
        )

    def take(ref, sem):
        pltpu.make_async_copy(ref, ref, sem).wait()

    smalls = [
        pltpu.make_async_copy(src, dst, in_sem.at[i])
        for i, (src, dst) in enumerate(
            [
                (start_hbm, start_ref),
                (ptr_hbm, ptr_ref),
                (cpart_hbm, cpart_ref),
                (cloc_hbm, cloc_ref),
                (halo_hbm, halo_ref),
            ]
        )
    ]
    for load in smalls:
        load.start()

    barrier = pltpu.get_barrier_semaphore()
    for i, j in plane:
        pl.semaphore_signal(barrier, inc=1, device_id=(twin(i), beside(j)), device_id_type=MESH)
    others = []
    for offset in range(1, n_dom):
        others.append(offset)
    for offset in others:
        pl.semaphore_signal(barrier, inc=1, device_id=(up(offset), me), device_id_type=MESH)

    n_loads = slots // CHUNK
    loads = [
        pltpu.make_async_copy(
            tiles_ref.at[0, pl.ds(c * CHUNK, CHUNK)], raw.at[pl.ds(c * CHUNK, CHUNK)], tile_sem.at[c]
        )
        for c in range(n_loads)
    ]
    for load in loads:
        load.start()

    def put_own(a, c, values):
        for b in range(block_rows):
            part(a, c)[me * block_rows + b] = values[:, b * block : (b + 1) * block]

    def near_start(a, c):
        mine = part(a, c).at[pl.ds(me * block_rows, block_rows)]
        for j in range(1, n_group):
            remote(mine, mine, x_send.at[a, c], f_recv.at[a, c], (own, beside(j))).start()

    def far_start(a, c):
        take(part(a, c).at[pl.ds(0, in_part - block_rows)], f_recv.at[a, c])
        for o in doms:
            for h in range(halo):
                stage_ref[a, c, o, h] = part(a, c)[halo_ref[0, h, up(o)]]
            remote(
                stage_ref.at[a, c, o],
                border(a, c).at[pl.ds(own * halo, halo)],
                x_send.at[a, c],
                z_recv.at[a, c],
                (up(o), me),
            ).start()

    def far_wait(a, c):
        take(border(a, c).at[pl.ds(0, (n_dom - 1) * halo)], z_recv.at[a, c])

    def sends_wait(a, c):
        for _ in range(n_group - 1):
            take(part(a, c).at[pl.ds(0, block_rows)], x_send.at[a, c])
        for o in doms:
            take(stage_ref.at[a, c, o], x_send.at[a, c])

    def apply_graph(a, c):
        def pick(s):
            near, far = part(a, c)[near_ref[s]], border(a, c)[far_ref[s]]
            return jnp.where(cpart_ref[0, s] == own, near, far)

        total = jnp.zeros((ROWS, block), jnp.float32)
        for s in range(0, slots, 2):
            both = dot(jnp.concatenate([pick(s), pick(s + 1)], axis=0), tb[s // 2])
            total = total + both[:ROWS, :block]
            prod[s + 1] = total
            total = total + both[ROWS:, block:]
            prod[s + 2] = total
        out = []
        for r in range(block_rows):
            out.append((prod[ptr_ref[0, r + 1]] - prod[ptr_ref[0, r]]) * scale_ref[r : r + 1, :])
        return jnp.concatenate(out, axis=1)

    half = width // pair
    fold = half // 2

    def sum_one(t, value):
        for i in range(pair):
            packed = jnp.concatenate(
                [value[i * half : i * half + fold], value[i * half + fold : (i + 1) * half]], axis=1
            )
            g_src[t, i] = packed
        g_one[t, core * n_group + me] = g_src[t, core]
        for i, j in plane:
            remote(
                g_src.at[t, lax.rem(core + i, pair)],
                g_one.at[t, core * n_group + me],
                g_send.at[t],
                g_recv.at[t, 0],
                (twin(i), beside(j)),
            ).start()

    def sum_two(t):
        take(g_one.at[t, pl.ds(0, len(plane))], g_recv.at[t, 0])
        total = g_one[t, 0]
        for j in range(1, pair * n_group):
            total = total + g_one[t, j]
        g_two[t, own] = total
        for o in doms:
            remote(g_two.at[t, own], g_two.at[t, own], g_send.at[t], g_recv.at[t, 1], (up(o), me)).start()

    def sum_end(t):
        take(g_two.at[t, pl.ds(0, n_dom - 1)], g_recv.at[t, 1])
        pieces = []
        for i in range(pair):
            total = g_two[t, i]
            for j in range(i + pair, n_dom, pair):
                total = total + g_two[t, j]
            pieces += [total[:, :width], total[:, width:]]
        return jnp.concatenate(pieces, axis=0) * (1.0 / total_rows)

    def sum_sends(t):
        for _ in range(len(plane) + n_dom - 1):
            take(g_one.at[t, 0], g_send.at[t])

    smalls[0].wait()
    for c in range(n_chunk):
        put_own(0, c, start_ref[c * ROWS : (c + 1) * ROWS, :])
    pl.semaphore_wait(barrier, len(plane) + len(others))
    for c in range(n_chunk):
        near_start(0, c)
    for load in smalls[1:]:
        load.wait()
    for s in range(slots):
        here = cpart_ref[0, s] == own
        near_ref[s] = jnp.where(here, cloc_ref[0, s], 0)
        far_ref[s] = jnp.where(here, 0, cpart_ref[0, s] * halo + cloc_ref[0, s])
    for r in range(block_rows):
        count = jnp.full((1, block), ptr_ref[0, r + 1] - ptr_ref[0, r], jnp.int32).astype(jnp.float32)
        scale_ref[r : r + 1, :] = 1.0 / (4.0 * jnp.sqrt(block * count))
    prod[0] = jnp.zeros((ROWS, block), jnp.float32)

    def convert_group(c):
        loads[c].wait()

        def convert(i, carry):
            s = c * (CHUNK // 2) + i
            for k in range(2):
                tile = (raw[2 * s + k].astype(jnp.float32) - 7.5).astype(jnp.bfloat16)
                tb[s, :, k * block : (k + 1) * block] = jnp.transpose(tile)
            return carry

        lax.fori_loop(0, CHUNK // 2, convert, 0)

    for c in range(n_loads // 2):
        convert_group(c)
    for c in range(n_chunk):
        far_start(0, c)
    for c in range(n_loads // 2, n_loads):
        convert_group(c)

    inverse = None
    for a in range(n_apply):
        for c in range(n_chunk):
            far_wait(a, c)
            image = apply_graph(a, c)
            span = slice(c * ROWS, (c + 1) * ROWS)
            if a < ITERS:
                rounded = image.astype(jnp.bfloat16)
                put_own(a + 1, c, rounded)
                near_start(a + 1, c)
                bf_ref[a, span, :] = rounded
                if c >= LAG:
                    far_start(a + 1, c - LAG)
            if a >= 1:
                im_ref[a - 1, span, :] = image
            if a >= 1 and c == min(1, n_chunk - 1):
                sum_two(a - 1)
        if a < ITERS:
            for c in range(max(0, n_chunk - LAG), n_chunk):
                far_start(a + 1, c)
            sum_one(a, dot(bf_ref[a], bf_ref[a], ((1,), (1,))))
            if a == 1:
                inverse = factor_end(factor_steps(factor_start(sum_end(0)), 0, width))

    local = dot(im_ref[0], im_ref[1], ((1,), (1,)), precision=HIGH)
    sum_one(ITERS, local)
    gram = dot(inverse, dot(sum_end(1), inverse, ((1,), (1,)), precision=HIGHEST), precision=HIGHEST)
    state = factor_steps(factor_start(gram), 0, width // 2)
    sum_two(ITERS)
    whole = dot(factor_end(factor_steps(state, width // 2, width)), inverse, precision=HIGHEST)
    vec_ref[...] = dot(whole, im_ref[0], precision=HIGH).astype(jnp.bfloat16)
    for a in range(n_apply):
        for c in range(n_chunk):
            sends_wait(a, c)
    h = sum_end(ITERS)
    ritz_ref[...] = dot(whole, dot(h, whole, ((1,), (1,)), precision=HIGHEST), precision=HIGHEST)
    for t in range(n_apply):
        sum_sends(t)


def finish(vec_in, ritz_in, vec_out, ritz_out):
    vec_out[...] = vec_in[...]
    ritz_out[...] = ritz_in[...]


def solution(mesh):
    n_dom, n_group = mesh.shape["dom"], mesh.shape["group"]
    n_apply = ITERS + 1
    pair = 2 if n_dom % 2 == 0 else 1

    def step(start, tiles, row_ptr, col_part, col_local, halo_list):
        width, rows_dev = start.shape
        slots, block = tiles.shape[1], tiles.shape[2]
        halo = halo_list.shape[2]
        in_part = rows_dev // block * n_group
        halo_list = jnp.transpose(halo_list, (0, 2, 1))
        n_chunk = width // ROWS
        vmem = pl.BlockSpec(memory_space=pltpu.VMEM)
        dma = pltpu.SemaphoreType.DMA
        outs = (
            jax.ShapeDtypeStruct((width, rows_dev), jnp.bfloat16),
            jax.ShapeDtypeStruct((width, width), jnp.float32),
        )
        packed = (width // pair // 2, 2 * width)
        vectors, ritz = pl.pallas_call(
            functools.partial(kernel, n_dom, n_group, halo, rows_dev * n_dom * n_group),
            out_shape=outs,
            in_specs=[pl.BlockSpec(memory_space=pltpu.HBM)] * 6,
            out_specs=(vmem, vmem),
            scratch_shapes=[
                pltpu.VMEM(start.shape, start.dtype),
                pltpu.SMEM(row_ptr.shape, jnp.int32),
                pltpu.SMEM(col_part.shape, jnp.int32),
                pltpu.SMEM(col_local.shape, jnp.int32),
                pltpu.SMEM(halo_list.shape, jnp.int32),
                dma((5,)),
            ]
            + [pltpu.VMEM((in_part, ROWS, block), jnp.bfloat16)] * (n_apply * n_chunk)
            + [pltpu.VMEM((n_dom * halo, ROWS, block), jnp.bfloat16)] * (n_apply * n_chunk)
            + [
                pltpu.VMEM((n_apply, n_chunk, n_dom, halo, ROWS, block), jnp.bfloat16),
                pltpu.VMEM((slots, block, block), jnp.int32),
                pltpu.VMEM((slots // 2, block, 2 * block), jnp.bfloat16),
                pltpu.VMEM((slots + 1, ROWS, block), jnp.float32),
                pltpu.SMEM((slots,), jnp.int32),
                pltpu.SMEM((slots,), jnp.int32),
                pltpu.VMEM((rows_dev // block, block), jnp.float32),
                pltpu.VMEM((ITERS, width, rows_dev), jnp.bfloat16),
                pltpu.VMEM((2, width, rows_dev), jnp.float32),
                pltpu.VMEM((n_apply, pair) + packed, jnp.float32),
                pltpu.VMEM((n_apply, pair * n_group) + packed, jnp.float32),
                pltpu.VMEM((n_apply, n_dom) + packed, jnp.float32),
                dma((slots // CHUNK,)),
                dma((n_apply, n_chunk)),
                dma((n_apply, n_chunk)),
                dma((n_apply, n_chunk)),
                dma((n_apply, 2)),
                dma((n_apply,)),
            ],
            compiler_params=pltpu.CompilerParams(
                collective_id=0, has_side_effects=True, vmem_limit_bytes=67043328
            ),
        )(start, tiles, row_ptr, col_part, col_local, halo_list)
        return pl.pallas_call(finish, out_shape=outs, in_specs=[vmem, vmem], out_specs=(vmem, vmem))(vectors, ritz)

    return jax.shard_map(
        step,
        mesh=mesh,
        in_specs=(
            P(None, ("dom", "group")),
            P(("dom", "group"), None, None, None),
            P(("dom", "group"), None),
            P(("dom", "group"), None),
            P(("dom", "group"), None),
            P("dom", None, None),
        ),
        out_specs=(P(None, ("dom", "group")), P()),
        check_vma=False,
    )
```

```python
import functools

import jax
import jax.numpy as jnp
from jax import lax
from jax.experimental import pallas as pl
from jax.experimental.pallas import tpu as pltpu
from jax.sharding import PartitionSpec as P

ITERS = 2
MESH = pl.DeviceIdType.MESH
HIGH = lax.Precision.HIGH
CHUNK = 8
PANEL = 8
ROWS = 16
LAG = 1


def dot(a, b, dims=((1,), (0,)), precision=None):
    return lax.dot_general(a, b, (dims, ((), ())), precision=precision, preferred_element_type=jnp.float32)


def factor_start(gram):
    k = gram.shape[0]
    rows = lax.broadcasted_iota(jnp.int32, (k, k), 0)
    cols = lax.broadcasted_iota(jnp.int32, (k, k), 1)
    work = jnp.concatenate([gram, jnp.where(rows == cols, 1.0, 0.0).astype(jnp.float32)], axis=1)
    return work, jnp.ones(work.shape, jnp.float32)


def factor_steps(state, first, last):
    work, pivots = state
    row_ids = lax.broadcasted_iota(jnp.int32, work.shape, 0)
    for i in range(first, last, PANEL):
        cols = [jnp.broadcast_to(work[:, i + b : i + b + 1], work.shape) for b in range(PANEL)]
        rows = [work[i + b : i + b + 1, :] for b in range(PANEL)]
        for b in range(PANEL):
            pivot = cols[b][i + b : i + b + 1, :]
            inv = 1.0 / pivot
            pivots = jnp.where(row_ids == i + b, pivot, pivots)
            for c in range(b + 1, PANEL):
                ratio = cols[c][i + b : i + b + 1, :] * inv
                rows[c] = rows[c] - (cols[b][i + c : i + c + 1, :] * inv) * rows[b]
                cols[c] = cols[c] - cols[b] * ratio
            work = work - jnp.where(row_ids > i + b, cols[b], 0.0) * (rows[b] * inv)
    return work, pivots


def factor_end(state):
    work, pivots = state
    k = work.shape[0]
    return work[:, k:] * (1.0 / jnp.sqrt(pivots[:, k:]))


def kernel(n_dom, n_group, halo, total_rows, *refs):
    start_hbm, tiles_ref, ptr_hbm, cpart_hbm, cloc_hbm, halo_hbm, vec_ref, ritz_ref = refs[:8]
    start_ref, ptr_ref, cpart_ref, cloc_ref, halo_ref, in_sem = refs[8:14]
    refs = refs[14:]
    n_apply = ITERS + 1
    n_chunk = start_ref.shape[0] // ROWS
    parts, refs = refs[: n_apply * n_chunk], refs[n_apply * n_chunk :]
    halos, refs = refs[: n_apply * n_chunk], refs[n_apply * n_chunk :]
    stage_ref, raw, tb, prod, near_ref, far_ref, scale_ref, bf_ref, im_ref = refs[:9]
    g_src, g_one, g_two, tile_sem, f_recv, z_recv, x_send, g_recv, g_send = refs[9:]

    def part(a, c):
        return parts[a * n_chunk + c]

    def border(a, c):
        return halos[a * n_chunk + c]

    own = lax.axis_index("dom")
    me = lax.axis_index("group")
    slots, block = raw.shape[0], raw.shape[1]
    width = start_ref.shape[0]
    block_rows = start_ref.shape[1] // block
    in_part = block_rows * n_group
    pair = 2 if n_dom % 2 == 0 else 1
    core = lax.rem(own, pair)
    doms = []
    for step in range(n_dom // 2, 0, -1):
        doms.append(step)
        if n_dom - step != step:
            doms.append(n_dom - step)

    def up(offset):
        return lax.rem(own + offset, n_dom)

    def beside(offset):
        return lax.rem(me + offset, n_group)

    def twin(offset):
        return own - core + lax.rem(core + offset, pair)

    plane = [(i, j) for i in range(pair) for j in range(n_group) if i or j]

    def remote(src, dst, send_sem, recv_sem, device):
        return pltpu.make_async_remote_copy(
            src_ref=src, dst_ref=dst, send_sem=send_sem, recv_sem=recv_sem, device_id=device, device_id_type=MESH
        )

    def take(ref, sem):
        pltpu.make_async_copy(ref, ref, sem).wait()

    smalls = [
        pltpu.make_async_copy(src, dst, in_sem.at[i])
        for i, (src, dst) in enumerate(
            [
                (start_hbm, start_ref),
                (ptr_hbm, ptr_ref),
                (cpart_hbm, cpart_ref),
                (cloc_hbm, cloc_ref),
                (halo_hbm, halo_ref),
            ]
        )
    ]
    for load in smalls:
        load.start()

    barrier = pltpu.get_barrier_semaphore()
    for i, j in plane:
        pl.semaphore_signal(barrier, inc=1, device_id=(twin(i), beside(j)), device_id_type=MESH)
    others = []
    for offset in range(1, n_dom):
        others.append(offset)
    for offset in others:
        pl.semaphore_signal(barrier, inc=1, device_id=(up(offset), me), device_id_type=MESH)

    n_loads = slots // CHUNK
    loads = [
        pltpu.make_async_copy(
            tiles_ref.at[0, pl.ds(c * CHUNK, CHUNK)], raw.at[pl.ds(c * CHUNK, CHUNK)], tile_sem.at[c]
        )
        for c in range(n_loads)
    ]
    for load in loads:
        load.start()

    def put_own(a, c, values):
        for b in range(block_rows):
            part(a, c)[me * block_rows + b] = values[:, b * block : (b + 1) * block]

    def near_start(a, c):
        mine = part(a, c).at[pl.ds(me * block_rows, block_rows)]
        for j in range(1, n_group):
            remote(mine, mine, x_send.at[a, c], f_recv.at[a, c], (own, beside(j))).start()

    def far_start(a, c):
        take(part(a, c).at[pl.ds(0, in_part - block_rows)], f_recv.at[a, c])
        for o in doms:
            for h in range(halo):
                stage_ref[a, c, o, h] = part(a, c)[halo_ref[0, h, up(o)]]
            remote(
                stage_ref.at[a, c, o],
                border(a, c).at[pl.ds(own * halo, halo)],
                x_send.at[a, c],
                z_recv.at[a, c],
                (up(o), me),
            ).start()

    def far_wait(a, c):
        take(border(a, c).at[pl.ds(0, (n_dom - 1) * halo)], z_recv.at[a, c])

    def sends_wait(a, c):
        take(part(a, c).at[pl.ds(0, in_part - block_rows)], x_send.at[a, c])
        take(border(a, c).at[pl.ds(0, (n_dom - 1) * halo)], x_send.at[a, c])

    def apply_graph(a, c):
        def pick(s):
            near, far = part(a, c)[near_ref[s]], border(a, c)[far_ref[s]]
            return jnp.where(cpart_ref[0, s] == own, near, far)

        total = jnp.zeros((ROWS, block), jnp.float32)
        for s in range(0, slots, 2):
            both = dot(jnp.concatenate([pick(s), pick(s + 1)], axis=0), tb[s // 2])
            total = total + both[:ROWS, :block]
            prod[s + 1] = total
            total = total + both[ROWS:, block:]
            prod[s + 2] = total
        out = []
        for r in range(block_rows):
            out.append((prod[ptr_ref[0, r + 1]] - prod[ptr_ref[0, r]]) * scale_ref[r : r + 1, :])
        return jnp.concatenate(out, axis=1)

    half = width // pair
    fold = half // 2

    def sum_one(t, value):
        for i in range(pair):
            packed = jnp.concatenate(
                [value[i * half : i * half + fold], value[i * half + fold : (i + 1) * half]], axis=1
            )
            g_src[t, i] = packed
        g_one[t, core * n_group + me] = g_src[t, core]
        for i, j in plane:
            remote(
                g_src.at[t, lax.rem(core + i, pair)],
                g_one.at[t, core * n_group + me],
                g_send.at[t],
                g_recv.at[t, 0],
                (twin(i), beside(j)),
            ).start()

    def sum_two(t):
        take(g_one.at[t, pl.ds(0, len(plane))], g_recv.at[t, 0])
        total = g_one[t, 0]
        for j in range(1, pair * n_group):
            total = total + g_one[t, j]
        g_two[t, own] = total
        for o in doms:
            remote(g_two.at[t, own], g_two.at[t, own], g_send.at[t], g_recv.at[t, 1], (up(o), me)).start()

    def sum_end(t):
        take(g_two.at[t, pl.ds(0, n_dom - 1)], g_recv.at[t, 1])
        pieces = []
        for i in range(pair):
            total = g_two[t, i]
            for j in range(i + pair, n_dom, pair):
                total = total + g_two[t, j]
            pieces += [total[:, :width], total[:, width:]]
        return jnp.concatenate(pieces, axis=0) * (1.0 / total_rows)

    def sum_sends(t):
        take(g_one.at[t, pl.ds(0, len(plane))], g_send.at[t])
        take(g_two.at[t, pl.ds(0, n_dom - 1)], g_send.at[t])

    smalls[0].wait()
    for c in range(n_chunk):
        put_own(0, c, start_ref[c * ROWS : (c + 1) * ROWS, :])
    pl.semaphore_wait(barrier, len(plane) + len(others))
    for c in range(n_chunk):
        near_start(0, c)
    for load in smalls[1:]:
        load.wait()
    for s in range(slots):
        here = cpart_ref[0, s] == own
        near_ref[s] = jnp.where(here, cloc_ref[0, s], 0)
        far_ref[s] = jnp.where(here, 0, cpart_ref[0, s] * halo + cloc_ref[0, s])
    for r in range(block_rows):
        count = jnp.full((1, block), ptr_ref[0, r + 1] - ptr_ref[0, r], jnp.int32).astype(jnp.float32)
        scale_ref[r : r + 1, :] = 1.0 / (4.0 * jnp.sqrt(block * count))
    prod[0] = jnp.zeros((ROWS, block), jnp.float32)

    def convert_group(c):
        loads[c].wait()

        def convert(i, carry):
            s = c * (CHUNK // 2) + i
            for k in range(2):
                tile = (raw[2 * s + k].astype(jnp.float32) - 7.5).astype(jnp.bfloat16)
                tb[s, :, k * block : (k + 1) * block] = jnp.transpose(tile)
            return carry

        lax.fori_loop(0, CHUNK // 2, convert, 0)

    for c in range(n_loads // 2):
        convert_group(c)
    for c in range(n_chunk):
        far_start(0, c)
    for c in range(n_loads // 2, n_loads):
        convert_group(c)

    inverse = None
    for a in range(n_apply):
        for c in range(n_chunk):
            far_wait(a, c)
            image = apply_graph(a, c)
            span = slice(c * ROWS, (c + 1) * ROWS)
            if a < ITERS:
                rounded = image.astype(jnp.bfloat16)
                put_own(a + 1, c, rounded)
                near_start(a + 1, c)
                bf_ref[a, span, :] = rounded
                if c >= LAG:
                    far_start(a + 1, c - LAG)
            if a >= 1:
                im_ref[a - 1, span, :] = image
            if a >= 1:
                sends_wait(a - 1, c)
            if a >= 1 and c == min(1, n_chunk - 1):
                sum_two(a - 1)
        if a < ITERS:
            for c in range(max(0, n_chunk - LAG), n_chunk):
                far_start(a + 1, c)
            sum_one(a, dot(bf_ref[a], bf_ref[a], ((1,), (1,))))
            if a == 1:
                inverse = factor_end(factor_steps(factor_start(sum_end(0)), 0, width))

    local = dot(im_ref[0], im_ref[1], ((1,), (1,)), precision=HIGH)
    sum_one(ITERS, local)
    gram = dot(inverse, dot(sum_end(1), inverse, ((1,), (1,)), precision=HIGH), precision=HIGH)
    state = factor_steps(factor_start(gram), 0, width // 2)
    sum_two(ITERS)
    whole = dot(factor_end(factor_steps(state, width // 2, width)), inverse, precision=HIGH)
    vec_ref[...] = dot(whole, im_ref[0], precision=HIGH).astype(jnp.bfloat16)
    for c in range(n_chunk):
        sends_wait(ITERS, c)
    h = sum_end(ITERS)
    ritz_ref[...] = dot(whole, dot(h, whole, ((1,), (1,)), precision=HIGH), precision=HIGH)
    for t in range(n_apply):
        sum_sends(t)


def finish(vec_in, ritz_in, vec_out, ritz_out):
    vec_out[...] = vec_in[...]
    ritz_out[...] = ritz_in[...]


def solution(mesh):
    n_dom, n_group = mesh.shape["dom"], mesh.shape["group"]
    n_apply = ITERS + 1
    pair = 2 if n_dom % 2 == 0 else 1

    def step(start, tiles, row_ptr, col_part, col_local, halo_list):
        width, rows_dev = start.shape
        slots, block = tiles.shape[1], tiles.shape[2]
        halo = halo_list.shape[2]
        in_part = rows_dev // block * n_group
        halo_list = jnp.transpose(halo_list, (0, 2, 1))
        n_chunk = width // ROWS
        vmem = pl.BlockSpec(memory_space=pltpu.VMEM)
        dma = pltpu.SemaphoreType.DMA
        outs = (
            jax.ShapeDtypeStruct((width, rows_dev), jnp.bfloat16),
            jax.ShapeDtypeStruct((width, width), jnp.float32),
        )
        packed = (width // pair // 2, 2 * width)
        vectors, ritz = pl.pallas_call(
            functools.partial(kernel, n_dom, n_group, halo, rows_dev * n_dom * n_group),
            out_shape=outs,
            in_specs=[pl.BlockSpec(memory_space=pltpu.HBM)] * 6,
            out_specs=(vmem, vmem),
            scratch_shapes=[
                pltpu.VMEM(start.shape, start.dtype),
                pltpu.SMEM(row_ptr.shape, jnp.int32),
                pltpu.SMEM(col_part.shape, jnp.int32),
                pltpu.SMEM(col_local.shape, jnp.int32),
                pltpu.SMEM(halo_list.shape, jnp.int32),
                dma((5,)),
            ]
            + [pltpu.VMEM((in_part, ROWS, block), jnp.bfloat16)] * (n_apply * n_chunk)
            + [pltpu.VMEM((n_dom * halo, ROWS, block), jnp.bfloat16)] * (n_apply * n_chunk)
            + [
                pltpu.VMEM((n_apply, n_chunk, n_dom, halo, ROWS, block), jnp.bfloat16),
                pltpu.VMEM((slots, block, block), jnp.int32),
                pltpu.VMEM((slots // 2, block, 2 * block), jnp.bfloat16),
                pltpu.VMEM((slots + 1, ROWS, block), jnp.float32),
                pltpu.SMEM((slots,), jnp.int32),
                pltpu.SMEM((slots,), jnp.int32),
                pltpu.VMEM((rows_dev // block, block), jnp.float32),
                pltpu.VMEM((ITERS, width, rows_dev), jnp.bfloat16),
                pltpu.VMEM((2, width, rows_dev), jnp.float32),
                pltpu.VMEM((n_apply, pair) + packed, jnp.float32),
                pltpu.VMEM((n_apply, pair * n_group) + packed, jnp.float32),
                pltpu.VMEM((n_apply, n_dom) + packed, jnp.float32),
                dma((slots // CHUNK,)),
                dma((n_apply, n_chunk)),
                dma((n_apply, n_chunk)),
                dma((n_apply, n_chunk)),
                dma((n_apply, 2)),
                dma((n_apply,)),
            ],
            compiler_params=pltpu.CompilerParams(
                collective_id=0, has_side_effects=True, vmem_limit_bytes=67043328
            ),
        )(start, tiles, row_ptr, col_part, col_local, halo_list)
        return pl.pallas_call(finish, out_shape=outs, in_specs=[vmem, vmem], out_specs=(vmem, vmem))(vectors, ritz)

    return jax.shard_map(
        step,
        mesh=mesh,
        in_specs=(
            P(None, ("dom", "group")),
            P(("dom", "group"), None, None, None),
            P(("dom", "group"), None),
            P(("dom", "group"), None),
            P(("dom", "group"), None),
            P("dom", None, None),
        ),
        out_specs=(P(None, ("dom", "group")), P()),
        check_vma=False,
    )
```

```python
import functools

import jax
import jax.numpy as jnp
from jax import lax
from jax.experimental import pallas as pl
from jax.experimental.pallas import tpu as pltpu
from jax.sharding import PartitionSpec as P

ITERS = 2
MESH = pl.DeviceIdType.MESH
HIGH = lax.Precision.HIGH
CHUNK = 8
PANEL = 8
ROWS = 16
LAG = 1


def dot(a, b, dims=((1,), (0,)), precision=None):
    return lax.dot_general(a, b, (dims, ((), ())), precision=precision, preferred_element_type=jnp.float32)


def factor_start(gram):
    k = gram.shape[0]
    rows = lax.broadcasted_iota(jnp.int32, (k, k), 0)
    cols = lax.broadcasted_iota(jnp.int32, (k, k), 1)
    work = jnp.concatenate([gram, jnp.where(rows == cols, 1.0, 0.0).astype(jnp.float32)], axis=1)
    return work, jnp.ones(work.shape, jnp.float32)


def factor_steps(state, first, last):
    work, pivots = state
    row_ids = lax.broadcasted_iota(jnp.int32, work.shape, 0)
    for i in range(first, last, PANEL):
        cols = [jnp.broadcast_to(work[:, i + b : i + b + 1], work.shape) for b in range(PANEL)]
        rows = [work[i + b : i + b + 1, :] for b in range(PANEL)]
        for b in range(PANEL):
            pivot = cols[b][i + b : i + b + 1, :]
            inv = 1.0 / pivot
            pivots = jnp.where(row_ids == i + b, pivot, pivots)
            for c in range(b + 1, PANEL):
                ratio = cols[c][i + b : i + b + 1, :] * inv
                rows[c] = rows[c] - (cols[b][i + c : i + c + 1, :] * inv) * rows[b]
                cols[c] = cols[c] - cols[b] * ratio
            work = work - jnp.where(row_ids > i + b, cols[b], 0.0) * (rows[b] * inv)
    return work, pivots


def factor_end(state):
    work, pivots = state
    k = work.shape[0]
    return work[:, k:] * (1.0 / jnp.sqrt(pivots[:, k:]))


def kernel(n_dom, n_group, halo, total_rows, *refs):
    start_hbm, tiles_ref, ptr_hbm, cpart_hbm, cloc_hbm, halo_hbm, vec_ref, ritz_ref = refs[:8]
    start_ref, ptr_ref, cpart_ref, cloc_ref, halo_ref, in_sem = refs[8:14]
    refs = refs[14:]
    n_apply = ITERS + 1
    n_chunk = start_ref.shape[0] // ROWS
    parts, refs = refs[: n_apply * n_chunk], refs[n_apply * n_chunk :]
    halos, refs = refs[: n_apply * n_chunk], refs[n_apply * n_chunk :]
    stage_ref, raw, tb, prod, near_ref, far_ref, scale_ref, bf_ref, im_ref = refs[:9]
    g_src, g_one, g_two, tile_sem, f_recv, z_recv, x_send, g_recv, g_send, l_one, l_two, l_recv, l_send = refs[9:]

    def part(a, c):
        return parts[a * n_chunk + c]

    def border(a, c):
        return halos[a * n_chunk + c]

    own = lax.axis_index("dom")
    me = lax.axis_index("group")
    slots, block = raw.shape[0], raw.shape[1]
    width = start_ref.shape[0]
    block_rows = start_ref.shape[1] // block
    in_part = block_rows * n_group
    pair = 2 if n_dom % 2 == 0 else 1
    core = lax.rem(own, pair)
    doms = []
    for step in range(n_dom // 2, 0, -1):
        doms.append(step)
        if n_dom - step != step:
            doms.append(n_dom - step)

    def up(offset):
        return lax.rem(own + offset, n_dom)

    def beside(offset):
        return lax.rem(me + offset, n_group)

    def twin(offset):
        return own - core + lax.rem(core + offset, pair)

    plane = [(i, j) for i in range(pair) for j in range(n_group) if i or j]

    def remote(src, dst, send_sem, recv_sem, device):
        return pltpu.make_async_remote_copy(
            src_ref=src, dst_ref=dst, send_sem=send_sem, recv_sem=recv_sem, device_id=device, device_id_type=MESH
        )

    def take(ref, sem):
        pltpu.make_async_copy(ref, ref, sem).wait()

    smalls = [
        pltpu.make_async_copy(src, dst, in_sem.at[i])
        for i, (src, dst) in enumerate(
            [
                (start_hbm, start_ref),
                (ptr_hbm, ptr_ref),
                (cpart_hbm, cpart_ref),
                (cloc_hbm, cloc_ref),
                (halo_hbm, halo_ref),
            ]
        )
    ]
    for load in smalls:
        load.start()

    barrier = pltpu.get_barrier_semaphore()
    for i, j in plane:
        pl.semaphore_signal(barrier, inc=1, device_id=(twin(i), beside(j)), device_id_type=MESH)
    others = []
    for offset in range(1, n_dom):
        others.append(offset)
    for offset in others:
        pl.semaphore_signal(barrier, inc=1, device_id=(up(offset), me), device_id_type=MESH)

    n_loads = slots // CHUNK
    loads = [
        pltpu.make_async_copy(
            tiles_ref.at[0, pl.ds(c * CHUNK, CHUNK)], raw.at[pl.ds(c * CHUNK, CHUNK)], tile_sem.at[c]
        )
        for c in range(n_loads)
    ]
    for load in loads:
        load.start()

    def put_own(a, c, values):
        for b in range(block_rows):
            part(a, c)[me * block_rows + b] = values[:, b * block : (b + 1) * block]

    def near_start(a, c):
        mine = part(a, c).at[pl.ds(me * block_rows, block_rows)]
        for j in range(1, n_group):
            remote(mine, mine, x_send.at[a, c], f_recv.at[a, c], (own, beside(j))).start()

    def far_start(a, c):
        take(part(a, c).at[pl.ds(0, in_part - block_rows)], f_recv.at[a, c])
        for o in doms:
            for h in range(halo):
                stage_ref[a, c, o, h] = part(a, c)[halo_ref[0, h, up(o)]]
            remote(
                stage_ref.at[a, c, o],
                border(a, c).at[pl.ds(own * halo, halo)],
                x_send.at[a, c],
                z_recv.at[a, c],
                (up(o), me),
            ).start()

    def far_wait(a, c):
        take(border(a, c).at[pl.ds(0, (n_dom - 1) * halo)], z_recv.at[a, c])

    def sends_wait(a, c):
        take(part(a, c).at[pl.ds(0, in_part - block_rows)], x_send.at[a, c])
        take(border(a, c).at[pl.ds(0, (n_dom - 1) * halo)], x_send.at[a, c])

    def apply_graph(a, c):
        def pick(s):
            near, far = part(a, c)[near_ref[s]], border(a, c)[far_ref[s]]
            return jnp.where(cpart_ref[0, s] == own, near, far)

        total = jnp.zeros((ROWS, block), jnp.float32)
        for s in range(0, slots, 2):
            both = dot(jnp.concatenate([pick(s), pick(s + 1)], axis=0), tb[s // 2])
            total = total + both[:ROWS, :block]
            prod[s + 1] = total
            total = total + both[ROWS:, block:]
            prod[s + 2] = total
        out = []
        for r in range(block_rows):
            out.append((prod[ptr_ref[0, r + 1]] - prod[ptr_ref[0, r]]) * scale_ref[r : r + 1, :])
        return jnp.concatenate(out, axis=1)

    half = width // pair
    fold = half // 2

    def sum_one(t, value):
        for i in range(pair):
            packed = jnp.concatenate(
                [value[i * half : i * half + fold], value[i * half + fold : (i + 1) * half]], axis=1
            )
            g_src[t, i] = packed
        g_one[t, core * n_group + me] = g_src[t, core]
        for i, j in plane:
            remote(
                g_src.at[t, lax.rem(core + i, pair)],
                g_one.at[t, core * n_group + me],
                g_send.at[t],
                g_recv.at[t, 0],
                (twin(i), beside(j)),
            ).start()

    def sum_two(t):
        take(g_one.at[t, pl.ds(0, len(plane))], g_recv.at[t, 0])
        total = g_one[t, 0]
        for j in range(1, pair * n_group):
            total = total + g_one[t, j]
        g_two[t, own] = total
        for o in doms:
            remote(g_two.at[t, own], g_two.at[t, own], g_send.at[t], g_recv.at[t, 1], (up(o), me)).start()

    def sum_end(t):
        take(g_two.at[t, pl.ds(0, n_dom - 1)], g_recv.at[t, 1])
        pieces = []
        for i in range(pair):
            total = g_two[t, i]
            for j in range(i + pair, n_dom, pair):
                total = total + g_two[t, j]
            pieces += [total[:, :width], total[:, width:]]
        return jnp.concatenate(pieces, axis=0) * (1.0 / total_rows)

    def sum_sends(t):
        take(g_one.at[t, pl.ds(0, len(plane))], g_send.at[t])
        take(g_two.at[t, pl.ds(0, n_dom - 1)], g_send.at[t])

    lanes = block // ROWS
    tall = width // lanes

    def last_one(value):
        l_one[me] = jnp.concatenate([value[k * tall : (k + 1) * tall] for k in range(lanes)], axis=1)
        for j in range(1, n_group):
            remote(l_one.at[me], l_one.at[me], l_send.at[0], l_recv.at[0], (own, beside(j))).start()

    def last_two():
        take(l_one.at[pl.ds(0, n_group - 1)], l_recv.at[0])
        total = l_one[0]
        for j in range(1, n_group):
            total = total + l_one[j]
        l_two[own] = total
        for o in doms:
            remote(l_two.at[own], l_two.at[own], l_send.at[0], l_recv.at[1], (up(o), me)).start()

    def last_end():
        take(l_two.at[pl.ds(0, n_dom - 1)], l_recv.at[1])
        total = l_two[0]
        for j in range(1, n_dom):
            total = total + l_two[j]
        total = total * (1.0 / total_rows)
        return jnp.concatenate([total[:, k * ROWS : (k + 1) * ROWS] for k in range(lanes)], axis=0)

    def last_sends():
        take(l_one.at[pl.ds(0, n_group - 1)], l_send.at[0])
        take(l_two.at[pl.ds(0, n_dom - 1)], l_send.at[0])

    smalls[0].wait()
    for c in range(n_chunk):
        put_own(0, c, start_ref[c * ROWS : (c + 1) * ROWS, :])
    pl.semaphore_wait(barrier, len(plane) + len(others))
    for c in range(n_chunk):
        near_start(0, c)
    for load in smalls[1:]:
        load.wait()
    for s in range(slots):
        here = cpart_ref[0, s] == own
        near_ref[s] = jnp.where(here, cloc_ref[0, s], 0)
        far_ref[s] = jnp.where(here, 0, cpart_ref[0, s] * halo + cloc_ref[0, s])
    for r in range(block_rows):
        count = jnp.full((1, block), ptr_ref[0, r + 1] - ptr_ref[0, r], jnp.int32).astype(jnp.float32)
        scale_ref[r : r + 1, :] = 1.0 / (4.0 * jnp.sqrt(block * count))
    prod[0] = jnp.zeros((ROWS, block), jnp.float32)

    def convert_group(c):
        loads[c].wait()

        def convert(i, carry):
            s = c * (CHUNK // 2) + i
            for k in range(2):
                tile = (raw[2 * s + k].astype(jnp.float32) - 7.5).astype(jnp.bfloat16)
                tb[s, :, k * block : (k + 1) * block] = jnp.transpose(tile)
            return carry

        lax.fori_loop(0, CHUNK // 2, convert, 0)

    for c in range(n_loads // 2):
        convert_group(c)
    for c in range(n_chunk):
        far_start(0, c)
    for c in range(n_loads // 2, n_loads):
        convert_group(c)

    inverse = None
    early = width - ROWS
    for a in range(n_apply):
        for c in range(n_chunk):
            far_wait(a, c)
            image = apply_graph(a, c)
            span = slice(c * ROWS, (c + 1) * ROWS)
            if a < ITERS:
                rounded = image.astype(jnp.bfloat16)
                put_own(a + 1, c, rounded)
                near_start(a + 1, c)
                bf_ref[a, span, :] = rounded
                if c >= LAG:
                    far_start(a + 1, c - LAG)
            if a >= 1:
                im_ref[a - 1, span, :] = image
            if a >= 1:
                sends_wait(a - 1, c)
            if a >= 1 and c == min(1, n_chunk - 1):
                sum_two(a - 1)
            if a == ITERS and c == n_chunk - 2:
                first = dot(im_ref[0], im_ref[1, :early, :], ((1,), (1,)), precision=HIGH)
                sum_one(ITERS, jnp.concatenate([first, jnp.zeros((width, ROWS), jnp.float32)], axis=1))
        if a < ITERS:
            for c in range(max(0, n_chunk - LAG), n_chunk):
                far_start(a + 1, c)
            sum_one(a, dot(bf_ref[a], bf_ref[a], ((1,), (1,))))
            if a == 1:
                inverse = factor_end(factor_steps(factor_start(sum_end(0)), 0, width))

    last_one(dot(im_ref[0], im_ref[1, early:, :], ((1,), (1,)), precision=HIGH))
    sum_two(ITERS)
    gram = dot(inverse, dot(sum_end(1), inverse, ((1,), (1,)), precision=HIGH), precision=HIGH)
    state = factor_steps(factor_start(gram), 0, width // 2)
    last_two()
    whole = dot(factor_end(factor_steps(state, width // 2, width)), inverse, precision=HIGH)
    vec_ref[...] = dot(whole, im_ref[0], precision=HIGH).astype(jnp.bfloat16)
    for c in range(n_chunk):
        sends_wait(ITERS, c)
    h = jnp.concatenate([sum_end(ITERS)[:, :early], last_end()], axis=1)
    ritz_ref[...] = dot(whole, dot(h, whole, ((1,), (1,)), precision=HIGH), precision=HIGH)
    last_sends()
    for t in range(n_apply):
        sum_sends(t)


def finish(vec_in, ritz_in, vec_out, ritz_out):
    vec_out[...] = vec_in[...]
    ritz_out[...] = ritz_in[...]


def solution(mesh):
    n_dom, n_group = mesh.shape["dom"], mesh.shape["group"]
    n_apply = ITERS + 1
    pair = 2 if n_dom % 2 == 0 else 1

    def step(start, tiles, row_ptr, col_part, col_local, halo_list):
        width, rows_dev = start.shape
        slots, block = tiles.shape[1], tiles.shape[2]
        halo = halo_list.shape[2]
        in_part = rows_dev // block * n_group
        halo_list = jnp.transpose(halo_list, (0, 2, 1))
        n_chunk = width // ROWS
        vmem = pl.BlockSpec(memory_space=pltpu.VMEM)
        dma = pltpu.SemaphoreType.DMA
        outs = (
            jax.ShapeDtypeStruct((width, rows_dev), jnp.bfloat16),
            jax.ShapeDtypeStruct((width, width), jnp.float32),
        )
        packed = (width // pair // 2, 2 * width)
        vectors, ritz = pl.pallas_call(
            functools.partial(kernel, n_dom, n_group, halo, rows_dev * n_dom * n_group),
            out_shape=outs,
            in_specs=[pl.BlockSpec(memory_space=pltpu.HBM)] * 6,
            out_specs=(vmem, vmem),
            scratch_shapes=[
                pltpu.VMEM(start.shape, start.dtype),
                pltpu.SMEM(row_ptr.shape, jnp.int32),
                pltpu.SMEM(col_part.shape, jnp.int32),
                pltpu.SMEM(col_local.shape, jnp.int32),
                pltpu.SMEM(halo_list.shape, jnp.int32),
                dma((5,)),
            ]
            + [pltpu.VMEM((in_part, ROWS, block), jnp.bfloat16)] * (n_apply * n_chunk)
            + [pltpu.VMEM((n_dom * halo, ROWS, block), jnp.bfloat16)] * (n_apply * n_chunk)
            + [
                pltpu.VMEM((n_apply, n_chunk, n_dom, halo, ROWS, block), jnp.bfloat16),
                pltpu.VMEM((slots, block, block), jnp.int32),
                pltpu.VMEM((slots // 2, block, 2 * block), jnp.bfloat16),
                pltpu.VMEM((slots + 1, ROWS, block), jnp.float32),
                pltpu.SMEM((slots,), jnp.int32),
                pltpu.SMEM((slots,), jnp.int32),
                pltpu.VMEM((rows_dev // block, block), jnp.float32),
                pltpu.VMEM((ITERS, width, rows_dev), jnp.bfloat16),
                pltpu.VMEM((2, width, rows_dev), jnp.float32),
                pltpu.VMEM((n_apply, pair) + packed, jnp.float32),
                pltpu.VMEM((n_apply, pair * n_group) + packed, jnp.float32),
                pltpu.VMEM((n_apply, n_dom) + packed, jnp.float32),
                dma((slots // CHUNK,)),
                dma((n_apply, n_chunk)),
                dma((n_apply, n_chunk)),
                dma((n_apply, n_chunk)),
                dma((n_apply, 2)),
                dma((n_apply,)),
                pltpu.VMEM((n_group, width * ROWS // block, block), jnp.float32),
                pltpu.VMEM((n_dom, width * ROWS // block, block), jnp.float32),
                dma((2,)),
                dma((1,)),
            ],
            compiler_params=pltpu.CompilerParams(
                collective_id=0, has_side_effects=True, vmem_limit_bytes=67043328
            ),
        )(start, tiles, row_ptr, col_part, col_local, halo_list)
        return pl.pallas_call(finish, out_shape=outs, in_specs=[vmem, vmem], out_specs=(vmem, vmem))(vectors, ritz)

    return jax.shard_map(
        step,
        mesh=mesh,
        in_specs=(
            P(None, ("dom", "group")),
            P(("dom", "group"), None, None, None),
            P(("dom", "group"), None),
            P(("dom", "group"), None),
            P(("dom", "group"), None),
            P("dom", None, None),
        ),
        out_specs=(P(None, ("dom", "group")), P()),
        check_vma=False,
    )
```

```python
import functools

import jax
import jax.numpy as jnp
from jax import lax
from jax.experimental import pallas as pl
from jax.experimental.pallas import tpu as pltpu
from jax.sharding import PartitionSpec as P

ITERS = 2
MESH = pl.DeviceIdType.MESH
HIGH = lax.Precision.HIGH
HIGHEST = lax.Precision.HIGHEST
CHUNK = 8
PANEL = 8
ROWS = 16
LAG = 1


def dot(a, b, dims=((1,), (0,)), precision=None):
    return lax.dot_general(a, b, (dims, ((), ())), precision=precision, preferred_element_type=jnp.float32)


def factor_start(gram):
    k = gram.shape[0]
    rows = lax.broadcasted_iota(jnp.int32, (k, k), 0)
    cols = lax.broadcasted_iota(jnp.int32, (k, k), 1)
    work = jnp.concatenate([gram, jnp.where(rows == cols, 1.0, 0.0).astype(jnp.float32)], axis=1)
    return work, jnp.ones(work.shape, jnp.float32)


def factor_steps(state, first, last):
    work, pivots = state
    row_ids = lax.broadcasted_iota(jnp.int32, work.shape, 0)
    for i in range(first, last, PANEL):
        cols = [jnp.broadcast_to(work[:, i + b : i + b + 1], work.shape) for b in range(PANEL)]
        rows = [work[i + b : i + b + 1, :] for b in range(PANEL)]
        for b in range(PANEL):
            pivot = cols[b][i + b : i + b + 1, :]
            inv = 1.0 / pivot
            pivots = jnp.where(row_ids == i + b, pivot, pivots)
            for c in range(b + 1, PANEL):
                ratio = cols[c][i + b : i + b + 1, :] * inv
                rows[c] = rows[c] - (cols[b][i + c : i + c + 1, :] * inv) * rows[b]
                cols[c] = cols[c] - cols[b] * ratio
            work = work - jnp.where(row_ids > i + b, cols[b], 0.0) * (rows[b] * inv)
    return work, pivots


def factor_end(state):
    work, pivots = state
    k = work.shape[0]
    return work[:, k:] * (1.0 / jnp.sqrt(pivots[:, k:]))


def kernel(n_dom, n_group, halo, total_rows, *refs):
    start_hbm, tiles_ref, ptr_hbm, cpart_hbm, cloc_hbm, halo_hbm, vec_ref, ritz_ref = refs[:8]
    start_ref, ptr_ref, cpart_ref, cloc_ref, halo_ref, in_sem = refs[8:14]
    refs = refs[14:]
    n_apply = ITERS + 1
    n_chunk = start_ref.shape[0] // ROWS
    parts, refs = refs[: n_apply * n_chunk], refs[n_apply * n_chunk :]
    halos, refs = refs[: n_apply * n_chunk], refs[n_apply * n_chunk :]
    stage_ref, raw, tb, prod, near_ref, far_ref, scale_ref, bf_ref, im_ref = refs[:9]
    g_src, g_one, g_two, tile_sem, f_recv, z_recv, x_send, g_recv, g_send, l_one, l_two, l_recv, l_send = refs[9:]

    def part(a, c):
        return parts[a * n_chunk + c]

    def border(a, c):
        return halos[a * n_chunk + c]

    own = lax.axis_index("dom")
    me = lax.axis_index("group")
    slots, block = raw.shape[0], raw.shape[1]
    width = start_ref.shape[0]
    block_rows = start_ref.shape[1] // block
    in_part = block_rows * n_group
    pair = 2 if n_dom % 2 == 0 else 1
    core = lax.rem(own, pair)
    doms = []
    for step in range(n_dom // 2, 0, -1):
        doms.append(step)
        if n_dom - step != step:
            doms.append(n_dom - step)

    def up(offset):
        return lax.rem(own + offset, n_dom)

    def beside(offset):
        return lax.rem(me + offset, n_group)

    def twin(offset):
        return own - core + lax.rem(core + offset, pair)

    plane = [(i, j) for i in range(pair) for j in range(n_group) if i or j]

    def remote(src, dst, send_sem, recv_sem, device):
        return pltpu.make_async_remote_copy(
            src_ref=src, dst_ref=dst, send_sem=send_sem, recv_sem=recv_sem, device_id=device, device_id_type=MESH
        )

    def take(ref, sem):
        pltpu.make_async_copy(ref, ref, sem).wait()

    smalls = [
        pltpu.make_async_copy(src, dst, in_sem.at[i])
        for i, (src, dst) in enumerate(
            [
                (start_hbm, start_ref),
                (ptr_hbm, ptr_ref),
                (cpart_hbm, cpart_ref),
                (cloc_hbm, cloc_ref),
                (halo_hbm, halo_ref),
            ]
        )
    ]
    for load in smalls:
        load.start()

    barrier = pltpu.get_barrier_semaphore()
    for i, j in plane:
        pl.semaphore_signal(barrier, inc=1, device_id=(twin(i), beside(j)), device_id_type=MESH)
    others = []
    for offset in range(1, n_dom):
        others.append(offset)
    for offset in others:
        pl.semaphore_signal(barrier, inc=1, device_id=(up(offset), me), device_id_type=MESH)

    n_loads = slots // CHUNK
    loads = [
        pltpu.make_async_copy(
            tiles_ref.at[0, pl.ds(c * CHUNK, CHUNK)], raw.at[pl.ds(c * CHUNK, CHUNK)], tile_sem.at[c]
        )
        for c in range(n_loads)
    ]
    for load in loads:
        load.start()

    def put_own(a, c, values):
        for b in range(block_rows):
            part(a, c)[me * block_rows + b] = values[:, b * block : (b + 1) * block]

    def near_start(a, c):
        mine = part(a, c).at[pl.ds(me * block_rows, block_rows)]
        for j in range(1, n_group):
            remote(mine, mine, x_send.at[a, c], f_recv.at[a, c], (own, beside(j))).start()

    def far_start(a, c):
        take(part(a, c).at[pl.ds(0, in_part - block_rows)], f_recv.at[a, c])
        for o in doms:
            for h in range(halo):
                stage_ref[a, c, o, h] = part(a, c)[halo_ref[0, h, up(o)]]
            remote(
                stage_ref.at[a, c, o],
                border(a, c).at[pl.ds(own * halo, halo)],
                x_send.at[a, c],
                z_recv.at[a, c],
                (up(o), me),
            ).start()

    def far_wait(a, c):
        take(border(a, c).at[pl.ds(0, (n_dom - 1) * halo)], z_recv.at[a, c])

    def sends_wait(a, c):
        take(part(a, c).at[pl.ds(0, in_part - block_rows)], x_send.at[a, c])
        take(border(a, c).at[pl.ds(0, (n_dom - 1) * halo)], x_send.at[a, c])

    def apply_graph(a, c):
        def pick(s):
            near, far = part(a, c)[near_ref[s]], border(a, c)[far_ref[s]]
            return jnp.where(cpart_ref[0, s] == own, near, far)

        total = jnp.zeros((ROWS, block), jnp.float32)
        for s in range(0, slots, 2):
            both = dot(jnp.concatenate([pick(s), pick(s + 1)], axis=0), tb[s // 2])
            total = total + both[:ROWS, :block]
            prod[s + 1] = total
            total = total + both[ROWS:, block:]
            prod[s + 2] = total
        out = []
        for r in range(block_rows):
            out.append((prod[ptr_ref[0, r + 1]] - prod[ptr_ref[0, r]]) * scale_ref[r : r + 1, :])
        return jnp.concatenate(out, axis=1)

    half = width // pair
    fold = half // 2

    def sum_one(t, value):
        for i in range(pair):
            packed = jnp.concatenate(
                [value[i * half : i * half + fold], value[i * half + fold : (i + 1) * half]], axis=1
            )
            g_src[t, i] = packed
        g_one[t, core * n_group + me] = g_src[t, core]
        for i, j in plane:
            remote(
                g_src.at[t, lax.rem(core + i, pair)],
                g_one.at[t, core * n_group + me],
                g_send.at[t],
                g_recv.at[t, 0],
                (twin(i), beside(j)),
            ).start()

    def sum_two(t):
        take(g_one.at[t, pl.ds(0, len(plane))], g_recv.at[t, 0])
        total = g_one[t, 0]
        for j in range(1, pair * n_group):
            total = total + g_one[t, j]
        g_two[t, own] = total
        for o in doms:
            remote(g_two.at[t, own], g_two.at[t, own], g_send.at[t], g_recv.at[t, 1], (up(o), me)).start()

    def sum_end(t):
        take(g_two.at[t, pl.ds(0, n_dom - 1)], g_recv.at[t, 1])
        pieces = []
        for i in range(pair):
            total = g_two[t, i]
            for j in range(i + pair, n_dom, pair):
                total = total + g_two[t, j]
            pieces += [total[:, :width], total[:, width:]]
        return jnp.concatenate(pieces, axis=0) * (1.0 / total_rows)

    def sum_sends(t):
        take(g_one.at[t, pl.ds(0, len(plane))], g_send.at[t])
        take(g_two.at[t, pl.ds(0, n_dom - 1)], g_send.at[t])

    lanes = block // ROWS
    tall = width // lanes

    def last_one(value):
        l_one[me] = jnp.concatenate([value[k * tall : (k + 1) * tall] for k in range(lanes)], axis=1)
        for j in range(1, n_group):
            remote(l_one.at[me], l_one.at[me], l_send.at[0], l_recv.at[0], (own, beside(j))).start()

    def last_two():
        take(l_one.at[pl.ds(0, n_group - 1)], l_recv.at[0])
        total = l_one[0]
        for j in range(1, n_group):
            total = total + l_one[j]
        l_two[own] = total
        for o in doms:
            remote(l_two.at[own], l_two.at[own], l_send.at[0], l_recv.at[1], (up(o), me)).start()

    def last_end():
        take(l_two.at[pl.ds(0, n_dom - 1)], l_recv.at[1])
        total = l_two[0]
        for j in range(1, n_dom):
            total = total + l_two[j]
        total = total * (1.0 / total_rows)
        return jnp.concatenate([total[:, k * ROWS : (k + 1) * ROWS] for k in range(lanes)], axis=0)

    def last_sends():
        take(l_one.at[pl.ds(0, n_group - 1)], l_send.at[0])
        take(l_two.at[pl.ds(0, n_dom - 1)], l_send.at[0])

    smalls[0].wait()
    for c in range(n_chunk):
        put_own(0, c, start_ref[c * ROWS : (c + 1) * ROWS, :])
    pl.semaphore_wait(barrier, len(plane) + len(others))
    for c in range(n_chunk):
        near_start(0, c)
    for load in smalls[1:]:
        load.wait()
    for s in range(slots):
        here = cpart_ref[0, s] == own
        near_ref[s] = jnp.where(here, cloc_ref[0, s], 0)
        far_ref[s] = jnp.where(here, 0, cpart_ref[0, s] * halo + cloc_ref[0, s])
    for r in range(block_rows):
        count = jnp.full((1, block), ptr_ref[0, r + 1] - ptr_ref[0, r], jnp.int32).astype(jnp.float32)
        scale_ref[r : r + 1, :] = 1.0 / (4.0 * jnp.sqrt(block * count))
    prod[0] = jnp.zeros((ROWS, block), jnp.float32)

    def convert_group(c):
        loads[c].wait()

        def convert(i, carry):
            s = c * (CHUNK // 2) + i
            for k in range(2):
                tile = (raw[2 * s + k].astype(jnp.float32) - 7.5).astype(jnp.bfloat16)
                tb[s, :, k * block : (k + 1) * block] = jnp.transpose(tile)
            return carry

        lax.fori_loop(0, CHUNK // 2, convert, 0)

    for c in range(n_loads // 2):
        convert_group(c)
    for c in range(n_chunk):
        far_start(0, c)
    for c in range(n_loads // 2, n_loads):
        convert_group(c)

    inverse = None
    early = width - ROWS
    for a in range(n_apply):
        for c in range(n_chunk):
            far_wait(a, c)
            image = apply_graph(a, c)
            span = slice(c * ROWS, (c + 1) * ROWS)
            if a < ITERS:
                rounded = image.astype(jnp.bfloat16)
                put_own(a + 1, c, rounded)
                near_start(a + 1, c)
                bf_ref[a, span, :] = rounded
                if c >= LAG:
                    far_start(a + 1, c - LAG)
            if a >= 1:
                im_ref[a - 1, span, :] = image
            if a >= 1:
                sends_wait(a - 1, c)
            if a >= 1 and c == min(1, n_chunk - 1):
                sum_two(a - 1)
            if a == ITERS and c == n_chunk - 2:
                first = dot(im_ref[0], im_ref[1, :early, :], ((1,), (1,)), precision=HIGH)
                sum_one(ITERS, jnp.concatenate([first, jnp.zeros((width, ROWS), jnp.float32)], axis=1))
        if a < ITERS:
            for c in range(max(0, n_chunk - LAG), n_chunk):
                far_start(a + 1, c)
            sum_one(a, dot(bf_ref[a], bf_ref[a], ((1,), (1,))))
            if a == 1:
                inverse = factor_end(factor_steps(factor_start(sum_end(0)), 0, width))

    last_one(dot(im_ref[0], im_ref[1, early:, :], ((1,), (1,)), precision=HIGH))
    sum_two(ITERS)
    gram = dot(inverse, dot(sum_end(1), inverse, ((1,), (1,)), precision=HIGHEST), precision=HIGHEST)
    state = factor_steps(factor_start(gram), 0, width // 2)
    last_two()
    whole = dot(factor_end(factor_steps(state, width // 2, width)), inverse, precision=HIGHEST)
    vec_ref[...] = dot(whole, im_ref[0], precision=HIGH).astype(jnp.bfloat16)
    for c in range(n_chunk):
        sends_wait(ITERS, c)
    h = jnp.concatenate([sum_end(ITERS)[:, :early], last_end()], axis=1)
    ritz_ref[...] = dot(whole, dot(h, whole, ((1,), (1,)), precision=HIGHEST), precision=HIGHEST)
    last_sends()
    for t in range(n_apply):
        sum_sends(t)


def finish(vec_in, ritz_in, vec_out, ritz_out):
    vec_out[...] = vec_in[...]
    ritz_out[...] = ritz_in[...]


def solution(mesh):
    n_dom, n_group = mesh.shape["dom"], mesh.shape["group"]
    n_apply = ITERS + 1
    pair = 2 if n_dom % 2 == 0 else 1

    def step(start, tiles, row_ptr, col_part, col_local, halo_list):
        width, rows_dev = start.shape
        slots, block = tiles.shape[1], tiles.shape[2]
        halo = halo_list.shape[2]
        in_part = rows_dev // block * n_group
        halo_list = jnp.transpose(halo_list, (0, 2, 1))
        n_chunk = width // ROWS
        vmem = pl.BlockSpec(memory_space=pltpu.VMEM)
        dma = pltpu.SemaphoreType.DMA
        outs = (
            jax.ShapeDtypeStruct((width, rows_dev), jnp.bfloat16),
            jax.ShapeDtypeStruct((width, width), jnp.float32),
        )
        packed = (width // pair // 2, 2 * width)
        vectors, ritz = pl.pallas_call(
            functools.partial(kernel, n_dom, n_group, halo, rows_dev * n_dom * n_group),
            out_shape=outs,
            in_specs=[pl.BlockSpec(memory_space=pltpu.HBM)] * 6,
            out_specs=(vmem, vmem),
            scratch_shapes=[
                pltpu.VMEM(start.shape, start.dtype),
                pltpu.SMEM(row_ptr.shape, jnp.int32),
                pltpu.SMEM(col_part.shape, jnp.int32),
                pltpu.SMEM(col_local.shape, jnp.int32),
                pltpu.SMEM(halo_list.shape, jnp.int32),
                dma((5,)),
            ]
            + [pltpu.VMEM((in_part, ROWS, block), jnp.bfloat16)] * (n_apply * n_chunk)
            + [pltpu.VMEM((n_dom * halo, ROWS, block), jnp.bfloat16)] * (n_apply * n_chunk)
            + [
                pltpu.VMEM((n_apply, n_chunk, n_dom, halo, ROWS, block), jnp.bfloat16),
                pltpu.VMEM((slots, block, block), jnp.int32),
                pltpu.VMEM((slots // 2, block, 2 * block), jnp.bfloat16),
                pltpu.VMEM((slots + 1, ROWS, block), jnp.float32),
                pltpu.SMEM((slots,), jnp.int32),
                pltpu.SMEM((slots,), jnp.int32),
                pltpu.VMEM((rows_dev // block, block), jnp.float32),
                pltpu.VMEM((ITERS, width, rows_dev), jnp.bfloat16),
                pltpu.VMEM((2, width, rows_dev), jnp.float32),
                pltpu.VMEM((n_apply, pair) + packed, jnp.float32),
                pltpu.VMEM((n_apply, pair * n_group) + packed, jnp.float32),
                pltpu.VMEM((n_apply, n_dom) + packed, jnp.float32),
                dma((slots // CHUNK,)),
                dma((n_apply, n_chunk)),
                dma((n_apply, n_chunk)),
                dma((n_apply, n_chunk)),
                dma((n_apply, 2)),
                dma((n_apply,)),
                pltpu.VMEM((n_group, width * ROWS // block, block), jnp.float32),
                pltpu.VMEM((n_dom, width * ROWS // block, block), jnp.float32),
                dma((2,)),
                dma((1,)),
            ],
            compiler_params=pltpu.CompilerParams(
                collective_id=0, has_side_effects=True, vmem_limit_bytes=67043328
            ),
        )(start, tiles, row_ptr, col_part, col_local, halo_list)
        return pl.pallas_call(finish, out_shape=outs, in_specs=[vmem, vmem], out_specs=(vmem, vmem))(vectors, ritz)

    return jax.shard_map(
        step,
        mesh=mesh,
        in_specs=(
            P(None, ("dom", "group")),
            P(("dom", "group"), None, None, None),
            P(("dom", "group"), None),
            P(("dom", "group"), None),
            P(("dom", "group"), None),
            P("dom", None, None),
        ),
        out_specs=(P(None, ("dom", "group")), P()),
        check_vma=False,
    )
```

```python
import functools

import jax
import jax.numpy as jnp
from jax import lax
from jax.experimental import pallas as pl
from jax.experimental.pallas import tpu as pltpu
from jax.sharding import PartitionSpec as P

ITERS = 2
MESH = pl.DeviceIdType.MESH
HIGH = lax.Precision.HIGH
CHUNK = 8
PANEL = 8
ROWS = 16
LAG = 1


def dot(a, b, dims=((1,), (0,)), precision=None):
    return lax.dot_general(a, b, (dims, ((), ())), precision=precision, preferred_element_type=jnp.float32)


def factor_start(gram):
    k = gram.shape[0]
    rows = lax.broadcasted_iota(jnp.int32, (k, k), 0)
    cols = lax.broadcasted_iota(jnp.int32, (k, k), 1)
    return [], jnp.concatenate([gram, jnp.where(rows == cols, 1.0, 0.0).astype(jnp.float32)], axis=1)


def factor_steps(state, first, last):
    done, work = state
    done = list(done)
    ids = lax.broadcasted_iota(jnp.int32, (PANEL, work.shape[1]), 0)
    for i in range(first, last, PANEL):
        cols = [jnp.broadcast_to(work[:, i + b : i + b + 1], work.shape) for b in range(PANEL)]
        rows = [work[b : b + 1, :] for b in range(PANEL)]
        tail = work[PANEL:, :]
        block = jnp.zeros(ids.shape, jnp.float32)
        pivots = jnp.ones(ids.shape, jnp.float32)
        for b in range(PANEL):
            pivot = cols[b][b : b + 1, :]
            inv = 1.0 / pivot
            block = jnp.where(ids == b, rows[b], block)
            pivots = jnp.where(ids == b, pivot, pivots)
            for c in range(b + 1, PANEL):
                ratio = cols[c][b : b + 1, :] * inv
                rows[c] = rows[c] - (cols[b][c : c + 1, :] * inv) * rows[b]
                cols[c] = cols[c] - cols[b] * ratio
            if tail.shape[0]:
                tail = tail - cols[b][PANEL:, :] * (rows[b] * inv)
        done.append(block * (1.0 / jnp.sqrt(pivots)))
        work = tail
    return done, work


def factor_end(state):
    rows = jnp.concatenate(state[0], axis=0)
    return rows[:, rows.shape[0] :]


def kernel(n_dom, n_group, halo, total_rows, *refs):
    start_hbm, tiles_ref, ptr_hbm, cpart_hbm, cloc_hbm, halo_hbm, vec_ref, ritz_ref = refs[:8]
    start_ref, ptr_ref, cpart_ref, cloc_ref, halo_ref, in_sem = refs[8:14]
    refs = refs[14:]
    n_apply = ITERS + 1
    n_chunk = start_ref.shape[0] // ROWS
    parts, refs = refs[: n_apply * n_chunk], refs[n_apply * n_chunk :]
    halos, refs = refs[: n_apply * n_chunk], refs[n_apply * n_chunk :]
    stage_ref, raw, tb, prod, near_ref, far_ref, scale_ref, bf_ref, im_ref = refs[:9]
    g_src, g_one, g_two, g_all, tile_sem, f_recv, z_recv, x_send, g_recv, g_send, l_one, l_two, l_recv, l_send = refs[9:]

    def part(a, c):
        return parts[a * n_chunk + c]

    def border(a, c):
        return halos[a * n_chunk + c]

    own = lax.axis_index("dom")
    me = lax.axis_index("group")
    slots, block = raw.shape[0], raw.shape[1]
    width = start_ref.shape[0]
    block_rows = start_ref.shape[1] // block
    in_part = block_rows * n_group
    pair = 2 if n_dom % 2 == 0 else 1
    core = lax.rem(own, pair)
    doms = []
    for step in range(n_dom // 2, 0, -1):
        doms.append(step)
        if n_dom - step != step:
            doms.append(n_dom - step)

    def up(offset):
        return lax.rem(own + offset, n_dom)

    def beside(offset):
        return lax.rem(me + offset, n_group)

    def twin(offset):
        return own - core + lax.rem(core + offset, pair)

    plane = [(i, j) for i in range(pair) for j in range(n_group) if i or j]

    def remote(src, dst, send_sem, recv_sem, device):
        return pltpu.make_async_remote_copy(
            src_ref=src, dst_ref=dst, send_sem=send_sem, recv_sem=recv_sem, device_id=device, device_id_type=MESH
        )

    def take(ref, sem):
        pltpu.make_async_copy(ref, ref, sem).wait()

    smalls = [
        pltpu.make_async_copy(src, dst, in_sem.at[i])
        for i, (src, dst) in enumerate(
            [
                (start_hbm, start_ref),
                (ptr_hbm, ptr_ref),
                (cpart_hbm, cpart_ref),
                (cloc_hbm, cloc_ref),
                (halo_hbm, halo_ref),
            ]
        )
    ]
    for load in smalls:
        load.start()

    barrier = pltpu.get_barrier_semaphore()
    for i, j in plane:
        pl.semaphore_signal(barrier, inc=1, device_id=(twin(i), beside(j)), device_id_type=MESH)
    others = []
    for offset in range(1, n_dom):
        others.append(offset)
    for offset in others:
        pl.semaphore_signal(barrier, inc=1, device_id=(up(offset), me), device_id_type=MESH)

    n_loads = slots // CHUNK
    loads = [
        pltpu.make_async_copy(
            tiles_ref.at[0, pl.ds(c * CHUNK, CHUNK)], raw.at[pl.ds(c * CHUNK, CHUNK)], tile_sem.at[c]
        )
        for c in range(n_loads)
    ]
    for load in loads:
        load.start()

    def put_own(a, c, values):
        for b in range(block_rows):
            part(a, c)[me * block_rows + b] = values[:, b * block : (b + 1) * block]

    def near_start(a, c):
        mine = part(a, c).at[pl.ds(me * block_rows, block_rows)]
        for j in range(1, n_group):
            remote(mine, mine, x_send.at[a, c], f_recv.at[a, c], (own, beside(j))).start()

    def far_start(a, c):
        take(part(a, c).at[pl.ds(0, in_part - block_rows)], f_recv.at[a, c])
        for o in doms:
            for h in range(halo):
                stage_ref[a, c, o, h] = part(a, c)[halo_ref[0, h, up(o)]]
            remote(
                stage_ref.at[a, c, o],
                border(a, c).at[pl.ds(own * halo, halo)],
                x_send.at[a, c],
                z_recv.at[a, c],
                (up(o), me),
            ).start()

    def far_wait(a, c):
        take(border(a, c).at[pl.ds(0, (n_dom - 1) * halo)], z_recv.at[a, c])

    def sends_wait(a, c):
        take(part(a, c).at[pl.ds(0, in_part - block_rows)], x_send.at[a, c])
        take(border(a, c).at[pl.ds(0, (n_dom - 1) * halo)], x_send.at[a, c])

    def apply_graph(a, c):
        def pick(s):
            near, far = part(a, c)[near_ref[s]], border(a, c)[far_ref[s]]
            return jnp.where(cpart_ref[0, s] == own, near, far)

        total = jnp.zeros((ROWS, block), jnp.float32)
        for s in range(0, slots, 2):
            both = dot(jnp.concatenate([pick(s), pick(s + 1)], axis=0), tb[s // 2])
            total = total + both[:ROWS, :block]
            prod[s + 1] = total
            total = total + both[ROWS:, block:]
            prod[s + 2] = total
        out = []
        for r in range(block_rows):
            out.append((prod[ptr_ref[0, r + 1]] - prod[ptr_ref[0, r]]) * scale_ref[r : r + 1, :])
        return jnp.concatenate(out, axis=1)

    half = width // pair
    fold = half // 2

    def sum_one(t, value):
        for i in range(pair):
            packed = jnp.concatenate(
                [value[i * half : i * half + fold], value[i * half + fold : (i + 1) * half]], axis=1
            )
            g_src[t, i] = packed
        g_one[t, core * n_group + me] = g_src[t, core]
        for i, j in plane:
            remote(
                g_src.at[t, lax.rem(core + i, pair)],
                g_one.at[t, core * n_group + me],
                g_send.at[t],
                g_recv.at[t, 0],
                (twin(i), beside(j)),
            ).start()

    def unpack(halves):
        out = []
        for total in halves:
            out += [total[:, :width], total[:, width:]]
        return jnp.concatenate(out, axis=0) * (1.0 / total_rows)

    def sum_two(t):
        take(g_one.at[t, pl.ds(0, len(plane))], g_recv.at[t, 0])
        total = g_one[t, 0]
        for j in range(1, pair * n_group):
            total = total + g_one[t, j]
        g_two[t, own] = total
        for o in doms if t == ITERS else range(pair, n_dom, pair):
            remote(g_two.at[t, own], g_two.at[t, own], g_send.at[t], g_recv.at[t, 1], (up(o), me)).start()

    def sum_three(t):
        take(g_two.at[t, pl.ds(0, n_dom // pair - 1)], g_recv.at[t, 1])
        total = g_two[t, core]
        for j in range(pair, n_dom, pair):
            total = total + g_two[t, core + j]
        g_all[t, core] = total
        for i in range(1, pair):
            remote(g_all.at[t, core], g_all.at[t, core], g_send.at[t], g_recv.at[t, 2], (twin(i), me)).start()

    def sum_end(t):
        if t < ITERS:
            if pair > 1:
                take(g_all.at[t, pl.ds(0, pair - 1)], g_recv.at[t, 2])
            return unpack([g_all[t, i] for i in range(pair)])
        take(g_two.at[t, pl.ds(0, n_dom - 1)], g_recv.at[t, 1])
        halves = []
        for i in range(pair):
            total = g_two[t, i]
            for j in range(i + pair, n_dom, pair):
                total = total + g_two[t, j]
            halves.append(total)
        return unpack(halves)

    def sum_sends(t):
        take(g_one.at[t, pl.ds(0, len(plane))], g_send.at[t])
        count = n_dom - 1 if t == ITERS else n_dom // pair + pair - 2
        take(g_two.at[t, pl.ds(0, count)], g_send.at[t])

    lanes = block // ROWS
    tall = width // lanes

    def last_one(value):
        l_one[me] = jnp.concatenate([value[k * tall : (k + 1) * tall] for k in range(lanes)], axis=1)
        for j in range(1, n_group):
            remote(l_one.at[me], l_one.at[me], l_send.at[0], l_recv.at[0], (own, beside(j))).start()

    def last_two():
        take(l_one.at[pl.ds(0, n_group - 1)], l_recv.at[0])
        total = l_one[0]
        for j in range(1, n_group):
            total = total + l_one[j]
        l_two[own] = total
        for o in doms:
            remote(l_two.at[own], l_two.at[own], l_send.at[0], l_recv.at[1], (up(o), me)).start()

    def last_end():
        take(l_two.at[pl.ds(0, n_dom - 1)], l_recv.at[1])
        total = l_two[0]
        for j in range(1, n_dom):
            total = total + l_two[j]
        total = total * (1.0 / total_rows)
        return jnp.concatenate([total[:, k * ROWS : (k + 1) * ROWS] for k in range(lanes)], axis=0)

    def last_sends():
        take(l_one.at[pl.ds(0, n_group - 1)], l_send.at[0])
        take(l_two.at[pl.ds(0, n_dom - 1)], l_send.at[0])

    smalls[0].wait()
    for c in range(n_chunk):
        put_own(0, c, start_ref[c * ROWS : (c + 1) * ROWS, :])
    pl.semaphore_wait(barrier, len(plane) + len(others))
    for c in range(n_chunk):
        near_start(0, c)
    for load in smalls[1:]:
        load.wait()
    for s in range(slots):
        here = cpart_ref[0, s] == own
        near_ref[s] = jnp.where(here, cloc_ref[0, s], 0)
        far_ref[s] = jnp.where(here, 0, cpart_ref[0, s] * halo + cloc_ref[0, s])
    for r in range(block_rows):
        count = jnp.full((1, block), ptr_ref[0, r + 1] - ptr_ref[0, r], jnp.int32).astype(jnp.float32)
        scale_ref[r : r + 1, :] = 1.0 / (4.0 * jnp.sqrt(block * count))
    prod[0] = jnp.zeros((ROWS, block), jnp.float32)

    def convert_group(c):
        loads[c].wait()

        def convert(i, carry):
            s = c * (CHUNK // 2) + i
            for k in range(2):
                tile = (raw[2 * s + k].astype(jnp.float32) - 7.5).astype(jnp.bfloat16)
                tb[s, :, k * block : (k + 1) * block] = jnp.transpose(tile)
            return carry

        lax.fori_loop(0, CHUNK // 2, convert, 0)

    for c in range(n_loads // 2):
        convert_group(c)
    for c in range(n_chunk):
        far_start(0, c)
    for c in range(n_loads // 2, n_loads):
        convert_group(c)

    inverse = None
    early = width - ROWS
    for a in range(n_apply):
        for c in range(n_chunk):
            far_wait(a, c)
            image = apply_graph(a, c)
            span = slice(c * ROWS, (c + 1) * ROWS)
            if a < ITERS:
                rounded = image.astype(jnp.bfloat16)
                put_own(a + 1, c, rounded)
                near_start(a + 1, c)
                bf_ref[a, span, :] = rounded
                if c >= LAG:
                    far_start(a + 1, c - LAG)
            if a >= 1:
                im_ref[a - 1, span, :] = image
            if a >= 1:
                sends_wait(a - 1, c)
            if a >= 1 and c == min(1, n_chunk - 1):
                sum_two(a - 1)
            if a == ITERS and c == n_chunk - 2:
                first = dot(im_ref[0], im_ref[1, :early, :], ((1,), (1,)), precision=HIGH)
                sum_one(ITERS, jnp.concatenate([first, jnp.zeros((width, ROWS), jnp.float32)], axis=1))
        if a < ITERS:
            for c in range(max(0, n_chunk - LAG), n_chunk):
                far_start(a + 1, c)
            if a == 1:
                sum_three(0)
            sum_one(a, dot(bf_ref[a], bf_ref[a], ((1,), (1,))))
            if a == 1:
                inverse = factor_end(factor_steps(factor_start(sum_end(0)), 0, width))

    last_one(dot(im_ref[0], im_ref[1, early:, :], ((1,), (1,)), precision=HIGH))
    sum_three(1)
    sum_two(ITERS)
    gram = dot(inverse, dot(sum_end(1), inverse, ((1,), (1,)), precision=HIGH), precision=HIGH)
    state = factor_steps(factor_start(gram), 0, width // 2)
    last_two()
    whole = dot(factor_end(factor_steps(state, width // 2, width)), inverse, precision=HIGH)
    vec_ref[...] = dot(whole, im_ref[0], precision=HIGH).astype(jnp.bfloat16)
    for c in range(n_chunk):
        sends_wait(ITERS, c)
    h = jnp.concatenate([sum_end(ITERS)[:, :early], last_end()], axis=1)
    ritz_ref[...] = dot(whole, dot(h, whole, ((1,), (1,)), precision=HIGH), precision=HIGH)
    last_sends()
    for t in range(n_apply):
        sum_sends(t)


def finish(vec_in, ritz_in, vec_out, ritz_out):
    vec_out[...] = vec_in[...]
    ritz_out[...] = ritz_in[...]


def solution(mesh):
    n_dom, n_group = mesh.shape["dom"], mesh.shape["group"]
    n_apply = ITERS + 1
    pair = 2 if n_dom % 2 == 0 else 1

    def step(start, tiles, row_ptr, col_part, col_local, halo_list):
        width, rows_dev = start.shape
        slots, block = tiles.shape[1], tiles.shape[2]
        halo = halo_list.shape[2]
        in_part = rows_dev // block * n_group
        halo_list = jnp.transpose(halo_list, (0, 2, 1))
        n_chunk = width // ROWS
        vmem = pl.BlockSpec(memory_space=pltpu.VMEM)
        dma = pltpu.SemaphoreType.DMA
        outs = (
            jax.ShapeDtypeStruct((width, rows_dev), jnp.bfloat16),
            jax.ShapeDtypeStruct((width, width), jnp.float32),
        )
        packed = (width // pair // 2, 2 * width)
        vectors, ritz = pl.pallas_call(
            functools.partial(kernel, n_dom, n_group, halo, rows_dev * n_dom * n_group),
            out_shape=outs,
            in_specs=[pl.BlockSpec(memory_space=pltpu.HBM)] * 6,
            out_specs=(vmem, vmem),
            scratch_shapes=[
                pltpu.VMEM(start.shape, start.dtype),
                pltpu.SMEM(row_ptr.shape, jnp.int32),
                pltpu.SMEM(col_part.shape, jnp.int32),
                pltpu.SMEM(col_local.shape, jnp.int32),
                pltpu.SMEM(halo_list.shape, jnp.int32),
                dma((5,)),
            ]
            + [pltpu.VMEM((in_part, ROWS, block), jnp.bfloat16)] * (n_apply * n_chunk)
            + [pltpu.VMEM((n_dom * halo, ROWS, block), jnp.bfloat16)] * (n_apply * n_chunk)
            + [
                pltpu.VMEM((n_apply, n_chunk, n_dom, halo, ROWS, block), jnp.bfloat16),
                pltpu.VMEM((slots, block, block), jnp.int32),
                pltpu.VMEM((slots // 2, block, 2 * block), jnp.bfloat16),
                pltpu.VMEM((slots + 1, ROWS, block), jnp.float32),
                pltpu.SMEM((slots,), jnp.int32),
                pltpu.SMEM((slots,), jnp.int32),
                pltpu.VMEM((rows_dev // block, block), jnp.float32),
                pltpu.VMEM((ITERS, width, rows_dev), jnp.bfloat16),
                pltpu.VMEM((2, width, rows_dev), jnp.float32),
                pltpu.VMEM((n_apply, pair) + packed, jnp.float32),
                pltpu.VMEM((n_apply, pair * n_group) + packed, jnp.float32),
                pltpu.VMEM((n_apply, n_dom) + packed, jnp.float32),
                pltpu.VMEM((ITERS, pair) + packed, jnp.float32),
                dma((slots // CHUNK,)),
                dma((n_apply, n_chunk)),
                dma((n_apply, n_chunk)),
                dma((n_apply, n_chunk)),
                dma((n_apply, 3)),
                dma((n_apply,)),
                pltpu.VMEM((n_group, width * ROWS // block, block), jnp.float32),
                pltpu.VMEM((n_dom, width * ROWS // block, block), jnp.float32),
                dma((2,)),
                dma((1,)),
            ],
            compiler_params=pltpu.CompilerParams(
                collective_id=0, has_side_effects=True, vmem_limit_bytes=67043328
            ),
        )(start, tiles, row_ptr, col_part, col_local, halo_list)
        return pl.pallas_call(finish, out_shape=outs, in_specs=[vmem, vmem], out_specs=(vmem, vmem))(vectors, ritz)

    return jax.shard_map(
        step,
        mesh=mesh,
        in_specs=(
            P(None, ("dom", "group")),
            P(("dom", "group"), None, None, None),
            P(("dom", "group"), None),
            P(("dom", "group"), None),
            P(("dom", "group"), None),
            P("dom", None, None),
        ),
        out_specs=(P(None, ("dom", "group")), P()),
        check_vma=False,
    )
```
